512 devices in a mesh: dp: 32 (over z, x), expert: 16 (over y, core).
Axes of the slice: x: 4, y: 8, z: 8, core: 2. Of those that a mesh axis runs over, the one named last changes fastest.
Arguments:
- tokens: bfloat16 [100352, 1024], P(('dp', 'expert')), may hold values from -6 to 6
- route_weight: bfloat16 [100352], P(('dp', 'expert')), may hold values from 0.29882812 to 1
- expert_ids: int32 [100352, 1], P(('dp', 'expert')), may hold values from 0 to 15; in each aligned block of 196 rows (0 to 195, 196 to 391, ...) at most 24 rows name the same one
- visible: int32 [2048, 49], P(('dp', 'expert')), may hold values from 0 to 195, as said below
- owner_map: int32 [2048], P(('dp', 'expert')), may hold values from 0 to 15, as said below
- norm_gain: float32 [1024], replicated, may hold values from 0.5 to 1.5
- expert_in: bfloat16 [16, 2048, 1024], P('expert', 'dp'), may hold values from -0.1875 to 0.1875
- expert_out: bfloat16 [16, 2048, 1024], P('expert', 'dp'), may hold values from -0.125 to 0.125
- final_gain: float32 [1024], replicated, may hold values from 0.5 to 1.5
- embed_weight: bfloat16 [1024, 512], replicated, may hold values from -0.1875 to 0.1875
- mask_token: bfloat16 [512], replicated, may hold values from -4 to 4
- decoder_pos: bfloat16 [196, 512], replicated, may hold values from -3 to 3
- decoder_gain: float32 [512], replicated, may hold values from 0.5 to 1.5
- attention_in: bfloat16 [512, 1536], replicated
- attention_out: bfloat16 [512, 512], replicated, may hold values from -0.25 to 0.25
Outputs:
- decoded_grid: bfloat16 [2048, 196, 512], P(('dp', 'expert'))
The draws below stay inside these ranges and needn't reach their ends.
Inputs may be any that keep to these rules, and one draw needn't show every extreme that they name: `expert_ids`: in each aligned block of 196 rows (the tokens of one device) no expert is named by more than 24 rows. `visible`: each row names 49 different positions. `owner_map`: the 4 images of an aligned block (one device) share one owner; in each aligned block of 64 images the 16 blocks have different owners.
All inputs are finite; a program needn't handle non-finite values.
Results may differ from the reference program's by a relative error of at most 0.009.
Values may be sent and summed in bfloat16 or wider, within the bound.
A program may use at most 64 MiB of HBM per device.

```python
import math
import jax
import jax.numpy as jnp
import numpy as np
from jax import lax

D = 1024
FF = 2048
HEADS = 16
HEAD_DIM = 32
DD = 512
GRID = 196
VIS = 49
IMG_DEV = 4
EXPERTS = 16
TOK_DEV = 196
IMAGES = 2048
TOKENS = 100352
CAP = 24
N_DP = 32
N_EXPERT = 16


def draw_visible(key, part):
    subkeys = jax.random.split(key, IMAGES)
    chosen = jax.vmap(lambda single: jax.random.permutation(single, GRID)[:VIS])(subkeys)
    return chosen.astype(jnp.int32)


def draw_owner_map(key, part):
    subkeys = jax.random.split(key, N_DP)
    orders = jax.vmap(lambda single: jax.random.permutation(single, N_EXPERT))(subkeys)
    return jnp.repeat(orders, IMG_DEV, axis=1).reshape(-1).astype(jnp.int32)


def draw_attention_in(key, part):
    base = jax.random.normal(key, (DD, 3 * DD), jnp.float32) * DD ** (-0.5)
    return base.astype(jnp.bfloat16)


def shard_levels(key, shape, cuts, least, largest):
    def one(dim, blocks):
        steps = jax.random.uniform(jax.random.fold_in(jax.random.fold_in(key, 6), dim), (blocks,), jnp.float32, least / len(cuts), largest / len(cuts))
        return jnp.repeat(jnp.exp(steps), shape[dim] // blocks).reshape((-1,) + (1,) * (len(shape) - dim - 1))

    level = one(*cuts[0])
    for cut in cuts[1:]:
        level = level * one(*cut)
    return level


def shared_out(own_key, own, number, rows, amount, top, bound, skew):
    order = jax.random.permutation(own_key, amount)
    crowded, ordinary = load_shares(amount, rows * top, bound, skew, True), load_shares(amount, rows * top, bound, skew, False)
    places = jnp.arange(amount)

    def named(sizes, rotation):
        used = int((sizes > 0).sum())
        fixed = max(1, used // 4)
        shifted = fixed + (places - fixed + rotation * (used - fixed)) % max(1, amount - fixed)
        return jnp.zeros((amount,), jnp.int32).at[order[jnp.where(places < fixed, places, shifted)]].set(jnp.asarray(sizes, jnp.int32))

    sizes = jnp.where(number % 4 == 0, named(crowded, number // 4), named(ordinary, number - number // 4 - 1))
    mixed = jax.random.permutation(jax.random.fold_in(own, 3), amount)
    donor, receiver = mixed[0:amount // 2 * 2:2], mixed[1:amount // 2 * 2:2]
    margin = jnp.minimum(sizes[donor] - 1, bound - sizes[receiver]) // 2
    margin = jnp.where((donor == order[0]) | (receiver == order[0]) | (sizes[receiver] == 0), 0, jnp.maximum(margin, 0))
    shifted = jax.random.randint(jax.random.fold_in(own, 4), (amount // 2,), 0, 1 << 20) % (margin + 1)
    sizes = sizes.at[donor].add(-shifted).at[receiver].add(shifted)
    items = jnp.searchsorted(jnp.cumsum(sizes), jnp.arange(rows * top), side="right").astype(jnp.int32)
    listing = items.reshape(top, rows).T
    listing = listing[jax.random.permutation(jax.random.fold_in(own, 1), rows)]
    rotation = jax.random.randint(jax.random.fold_in(own, 2), (rows, 1), 0, top)
    return jnp.take_along_axis(listing, (jnp.arange(top)[None, :] + rotation) % top, axis=1)


def load_shares(number_of, total, most, lean, full):
    portions = [(1 << 20) // math.isqrt(rank ** lean) + 1 for rank in range(1, number_of + 1)]
    largest = most if full else min(most, max(-(-total // number_of), total * portions[0] // sum(portions)))
    least = 1 if total - largest >= number_of - 1 else 0
    counts, surplus = [largest] + [least] * (number_of - 1), total - largest - least * (number_of - 1)
    while surplus > 0:
        free = [i for i in range(1, number_of) if counts[i] < largest] or [i for i in range(1, number_of) if counts[i] < most]
        whole, budget = sum([portions[i] for i in free]), surplus
        for i in free:
            more = min(most - counts[i], max(1, budget * portions[i] // whole), surplus)
            counts[i] = counts[i] + more
            surplus = surplus - more
    return np.array(counts)


def noise(key, shape, spread, most, pieces=(), kind=jnp.bfloat16):
    entries = jax.random.normal(key, shape, jnp.float32) * spread
    if len(pieces) > 0:
        entries = shard_levels(key, shape, pieces, -0.22, 0.18) * entries
    return jnp.clip(entries, min=-most, max=most).astype(kind)


def setup_inputs(seed: int = 0) -> dict:
    key_list = jax.random.split(jax.random.key(seed), 16)
    tokens = noise(key_list[0], (TOKENS, D), 1.0, 6.0, ((0, 512),))
    route_weight = jnp.clip(0.29882812 + 0.7011719 * jax.random.uniform(key_list[1], (TOKENS,), jnp.float32) ** shard_levels(key_list[1], (TOKENS,), ((0, 512),), -0.2, 0.2), 0.29882812, 1.0).astype(jnp.bfloat16)
    expert_ids_keys = jax.random.split(jax.random.fold_in(key_list[2], 1), TOKENS // TOK_DEV)
    expert_ids_turns = jax.random.permutation(jax.random.fold_in(key_list[2], 3), TOKENS // TOK_DEV)
    expert_ids = jax.vmap(lambda own, number: shared_out(jax.random.fold_in(key_list[2], 2), own, number, TOK_DEV, EXPERTS, 1, CAP, 1))(expert_ids_keys, expert_ids_turns).reshape((TOKENS, 1))
    visible = draw_visible(jax.random.fold_in(key_list[15], 71), 0)
    owner_map = draw_owner_map(jax.random.fold_in(key_list[15], 71), 0)
    norm_gain = jnp.clip(1.0 + 0.1 * jax.random.normal(key_list[5], (D,), jnp.float32), 0.5, 1.5)
    expert_in = noise(key_list[6], (EXPERTS, FF, D), D ** -0.5, 0.1875, ((0, 16), (1, 32)))
    expert_out = noise(key_list[7], (EXPERTS, FF, D), FF ** -0.5, 0.125, ((0, 16), (1, 32)))
    final_gain = jnp.clip(1.0 + 0.1 * jax.random.normal(key_list[8], (D,), jnp.float32), 0.5, 1.5)
    embed_weight = noise(key_list[9], (D, DD), D ** -0.5, 0.1875)
    mask_token = noise(key_list[10], (DD,), 1.0, 4.0)
    decoder_pos = noise(key_list[11], (GRID, DD), 0.5, 3.0)
    decoder_gain = jnp.clip(1.0 + 0.1 * jax.random.normal(key_list[12], (DD,), jnp.float32), 0.5, 1.5)
    attention_in = draw_attention_in(jax.random.fold_in(key_list[15], 71), 0)
    attention_out = noise(key_list[14], (DD, DD), DD ** -0.5, 0.25)
    return dict(tokens=tokens, route_weight=route_weight, expert_ids=expert_ids, visible=visible, owner_map=owner_map, norm_gain=norm_gain, expert_in=expert_in, expert_out=expert_out, final_gain=final_gain, embed_weight=embed_weight, mask_token=mask_token, decoder_pos=decoder_pos, decoder_gain=decoder_gain, attention_in=attention_in, attention_out=attention_out)


EPSILON = 1e-06

def layer_norm(values, factor):
    values = values.astype(jnp.float32)
    centered = values - lax.optimization_barrier(jnp.mean(values, axis=-1, keepdims=True))
    variance = lax.optimization_barrier(jnp.mean(centered * centered, axis=-1, keepdims=True))
    return centered * lax.rsqrt(variance + EPSILON) * factor.astype(jnp.float32)

def reference(tokens, route_weight, expert_ids, visible, owner_map, norm_gain, expert_in, expert_out, final_gain, embed_weight, mask_token, decoder_pos, decoder_gain, attention_in, attention_out):
    blocks = TOKENS // TOK_DEV
    token_expert = expert_ids[:, 0].reshape(blocks, TOK_DEV)
    onehot = (token_expert[:, :, None] == jnp.arange(EXPERTS, dtype=jnp.int32)[None, None, :]).astype(jnp.int32)
    earlier = lax.optimization_barrier(jnp.sum((jnp.cumsum(onehot, axis=1) - onehot) * onehot, axis=2))
    block_ids = jnp.arange(blocks, dtype=jnp.int32)[:, None]
    slot_index = ((token_expert * blocks + block_ids) * CAP + earlier).reshape(-1).astype(jnp.int32)
    slots = jnp.zeros((EXPERTS * blocks * CAP, D), jnp.bfloat16).at[slot_index].set(tokens)
    slot_weight = jnp.zeros((EXPERTS * blocks * CAP,), jnp.bfloat16).at[slot_index].set(route_weight)

    def one_expert(operands):
        inputs, scaling, first, second = operands
        normed = layer_norm(inputs, norm_gain).astype(jnp.bfloat16)
        hidden = jax.nn.gelu(jnp.dot(normed, first.T, preferred_element_type=jnp.float32)).astype(jnp.bfloat16)
        update = jnp.dot(hidden, second, preferred_element_type=jnp.float32)
        return (inputs.astype(jnp.float32) + scaling.astype(jnp.float32)[:, None] * update).astype(jnp.bfloat16)
    merged_slots = lax.map(one_expert, (slots.reshape(EXPERTS, blocks * CAP, D), slot_weight.reshape(EXPERTS, blocks * CAP), expert_in, expert_out))
    merged = merged_slots.reshape(EXPERTS * blocks * CAP, D)[slot_index]
    final_normed = layer_norm(merged, final_gain).astype(jnp.bfloat16)
    embedded = jnp.dot(final_normed, embed_weight, preferred_element_type=jnp.float32).astype(jnp.bfloat16)
    embedded = embedded.reshape(IMAGES // IMG_DEV, IMG_DEV, VIS, DD)
    places = visible.reshape(IMAGES // IMG_DEV, IMG_DEV, VIS)

    def decode(operands):
        image_rows, positions = operands
        placing = positions[:, :, None] == jnp.arange(GRID, dtype=jnp.int32)[None, None, :]
        covered = jnp.any(placing, axis=1)
        placed = jnp.einsum('ivg,ivd->igd', placing.astype(jnp.float32), image_rows.astype(jnp.float32))
        canvas = jnp.where(covered[:, :, None], placed, mask_token.astype(jnp.float32)[None, None, :])
        initial = canvas + decoder_pos.astype(jnp.float32)[None]
        dec_normed = layer_norm(initial, decoder_gain).astype(jnp.bfloat16)
        projected = jnp.dot(dec_normed.reshape(IMG_DEV * GRID, DD), attention_in, preferred_element_type=jnp.float32).astype(jnp.bfloat16)
        projected = projected.reshape(IMG_DEV, GRID, 3, HEADS, HEAD_DIM).astype(jnp.float32)
        queries = projected[:, :, 0]
        key_rows = projected[:, :, 1]
        value_rows = projected[:, :, 2]
        scores = jnp.einsum('iqhc,ikhc->ihqk', queries, key_rows) * HEAD_DIM ** (-0.5)
        weights = jax.nn.softmax(scores, axis=-1).astype(jnp.bfloat16)
        mixed = jnp.einsum('ihqk,ikhc->iqhc', weights.astype(jnp.float32), value_rows).astype(jnp.bfloat16)
        update = jnp.dot(mixed.reshape(IMG_DEV * GRID, DD), attention_out, preferred_element_type=jnp.float32)
        return (initial + update.reshape(IMG_DEV, GRID, DD)).astype(jnp.bfloat16)
    decoded = lax.map(decode, (embedded, places)).reshape(IMAGES, GRID, DD)
    image_index = jnp.arange(IMAGES, dtype=jnp.int32)
    group_size = N_EXPERT * IMG_DEV
    target = (image_index - image_index % group_size + owner_map * IMG_DEV + image_index % IMG_DEV).astype(jnp.int32)
    return jnp.zeros((IMAGES, GRID, DD), jnp.bfloat16).at[target].set(decoded)
```

```python
import heapq

import jax
import jax.numpy as jnp
from jax import lax
from jax.experimental import pallas as pl
from jax.experimental.pallas import tpu as pltpu
from jax.sharding import PartitionSpec as P

D = 1024
HEADS = 16
HEAD_DIM = 32
DD = 512
GRID = 196
VIS = 49
TOK = 196
EXPERTS = 16
CAP = 24
SLOT = 32
ROWS = EXPERTS * SLOT
WIDE = D + 128
NX = 4
NZ = 8
UNITS = 64
PART = 48
EPSILON = 1e-06
TOKENS_AT = 20.0


def layer_norm(values, factor):
    values = values.astype(jnp.float32)
    centered = values - jnp.mean(values, axis=-1, keepdims=True)
    variance = jnp.mean(centered * centered, axis=-1, keepdims=True)
    return centered * lax.rsqrt(variance + EPSILON) * factor


def a2_max(j, way):
    return 4 if (way == 1) == (j == 0) else 3


def b1_max(way):
    return 4 if way == 1 else 3


def b2_max(k, way):
    return 2 if (way == 1) == (k % 2 == 0) else 1


def a_from(j):
    return {0: None, 1: ("a1", 0), 2: ("a1", 2), 3: ("a1", 1)}[j]


def z_step(k, longest):
    return (1, k) if k <= longest else (-1, NZ - k)


def build_plan():
    need = {("a1", 0): None, ("a1", 1): None, ("a1", 2): ("a1", 0)}
    for way in (1, -1):
        for t in range(1, b1_max(way) + 1):
            need[("b1", way, t)] = None if t == 1 else ("b1", way, t - 1)
    for k in range(NZ):
        way0, t0 = z_step(k, b1_max(1))
        for way in (1, -1):
            for t in range(1, b2_max(k, way) + 1):
                first = None if k == 0 else ("b1", way0, t0)
                need[("b2", k, way, t)] = first if t == 1 else ("b2", k, way, t - 1)
    for j in range(NX):
        for way in (1, -1):
            for t in range(1, a2_max(j, way) + 1):
                need[("a2", j, way, t)] = a_from(j) if t == 1 else ("a2", j, way, t - 1)

    def link(copy):
        if copy[0] == "a1":
            return ("x", -1 if copy[1] == 1 else 1)
        if copy[0] == "b2":
            return ("x", copy[2])
        return ("z", copy[2] if copy[0] == "a2" else copy[1])

    free = {}
    arrivals = []

    def push(copy, now):
        took = 2.1 if copy[0][0] == "a" else 3.5
        begin = max(now, free.get(link(copy), 0.0))
        free[link(copy)] = begin + took
        heapq.heappush(arrivals, (begin + took + 1.5, len(order) + len(arrivals), copy))

    order = []
    initial = [c for c in need if need[c] is None]
    for copy in initial:
        push(copy, 0.0)
    while arrivals:
        now, _, copy = heapq.heappop(arrivals)
        nexts = [c for c in need if need[c] == copy]
        order.append((now, copy, nexts))
        for c in nexts:
            push(c, now)
    slabs = []
    for k in range(NZ):
        wants = set(("b2", k, way, t) for way in (1, -1) for t in range(1, b2_max(k, way) + 1))
        if k == 0:
            wants |= {("a1", 0), ("a1", 1), ("a1", 2)}
        else:
            wants.add(("b1",) + z_step(k, b1_max(1)))
            for j in range(NX):
                wants.add(("a2", j) + z_step(k, a2_max(j, 1)))
        slabs.append(wants)
    ids = {c: i for i, c in enumerate(need)}
    return initial, order, slabs, ids


def slots_of(ids_row, rows):
    lane = ids_row.shape[1]
    expert = lax.broadcasted_iota(jnp.int32, (EXPERTS, lane), 0)
    onehot = (expert == ids_row).astype(jnp.float32)
    before = (
        lax.broadcasted_iota(jnp.int32, (lane, lane), 0)
        < lax.broadcasted_iota(jnp.int32, (lane, lane), 1)
    ).astype(jnp.bfloat16)
    count = jnp.dot(onehot.astype(jnp.bfloat16), before, preferred_element_type=jnp.float32)
    earlier = jnp.sum(count * onehot, axis=0, keepdims=True).astype(jnp.int32)
    slot = ids_row * SLOT + earlier
    return (lax.broadcasted_iota(jnp.int32, (rows, lane), 0) == slot).astype(jnp.float32)


def gelu(value):
    inner = 0.7978845608028654 * (value + 0.044715 * (value * value * value))
    return 0.5 * value * (1.0 + jnp.tanh(inner))


def expert_kernel(
    tokens_ref,
    weight_ref,
    meta_ref,
    gain_ref,
    in_ref,
    out_ref,
    final_ref,
    embed_ref,
    rows_ref,
    own_meta_ref,
    w,
    tokens_pad,
    send,
    got,
    metas,
    normed,
    total,
    outgoing,
    back,
    local_sems,
    w_send,
    w_recv,
    t_send,
    t_recv,
    m_send,
    m_recv,
    o_send,
    o_recv,
):
    initial, order, slabs, ids = build_plan()
    dp = lax.axis_index("dp")
    me = lax.axis_index("expert")
    z, x = lax.div(dp, NX), lax.rem(dp, NX)

    def at_z(step):
        return lax.rem(z + (step + NZ), NZ)

    def at_x(step):
        return lax.rem(x + (step + NX), NX)

    own_in = pltpu.make_async_copy(in_ref.at[0], w.at[z, x, pl.ds(0, UNITS)], local_sems.at[0])
    own_out = pltpu.make_async_copy(
        out_ref.at[0], w.at[z, x, pl.ds(UNITS, UNITS)], local_sems.at[1]
    )
    own_in.start()
    own_out.start()
    barrier = pltpu.get_barrier_semaphore()
    for near in (
        at_z(0) * NX + at_x(1),
        at_z(0) * NX + at_x(-1),
        at_z(1) * NX + at_x(0),
        at_z(-1) * NX + at_x(0),
    ):
        pl.semaphore_signal(
            barrier, inc=1, device_id={"dp": near}, device_id_type=pl.DeviceIdType.MESH
        )
    for d in range(1, EXPERTS):
        pl.semaphore_signal(
            barrier,
            inc=1,
            device_id={"expert": lax.rem(me + d, EXPERTS)},
            device_id_type=pl.DeviceIdType.MESH,
        )
    got[:, CAP:SLOT, :] = jnp.zeros((EXPERTS, SLOT - CAP, WIDE), jnp.bfloat16)
    back[:, CAP:SLOT, :] = jnp.zeros((EXPERTS, SLOT - CAP, DD), jnp.bfloat16)
    own_in.wait()
    own_out.wait()
    pl.semaphore_wait(barrier, 4 + EXPERTS - 1)

    def weight_copy(copy, arriving):
        kind = copy[0]
        shift = 1 if arriving else 0
        if kind == "a1":
            step = -1 if copy[1] == 1 else 1
            first = 1 if copy[1] == 2 else 0
            zi, xi = z, at_x(-step * (first + shift))
            target = at_z(0) * NX + at_x(step)
        elif kind == "b2":
            _, k, step, t = copy
            zi, xi = at_z(-k), at_x(-step * (t - 1 + shift))
            target = at_z(0) * NX + at_x(step)
        else:
            step, t = copy[-2:]
            j = copy[1] if kind == "a2" else 0
            zi, xi = at_z(-step * (t - 1 + shift)), at_x(-j)
            target = at_z(step) * NX + at_x(0)
        part = pl.ds(0, PART) if kind[0] == "a" else pl.ds(PART, 2 * UNITS - PART)
        block = w.at[zi, xi, part]
        return pltpu.make_async_remote_copy(
            src_ref=block,
            dst_ref=block,
            send_sem=w_send.at[ids[copy]],
            recv_sem=w_recv.at[ids[copy]],
            device_id={"dp": target},
            device_id_type=pl.DeviceIdType.MESH,
        )

    def exchange(src, dst, send_sem, recv_sem, d, away):
        peer = lax.rem(me + d, EXPERTS)
        from_peer = lax.rem(me + (EXPERTS - d), EXPERTS)
        return pltpu.make_async_remote_copy(
            src_ref=src(peer),
            dst_ref=dst(me if away else from_peer),
            send_sem=send_sem.at[d],
            recv_sem=recv_sem.at[d],
            device_id={"expert": peer},
            device_id_type=pl.DeviceIdType.MESH,
        )

    def meta_copy(d, away):
        return exchange(lambda p: meta_ref, lambda p: metas.at[p], m_send, m_recv, d, away)

    def token_copy(d, away):
        return exchange(
            lambda p: send.at[p, pl.ds(0, CAP)],
            lambda p: got.at[p, pl.ds(0, CAP)],
            t_send,
            t_recv,
            d,
            away,
        )

    def back_copy(d, away):
        return exchange(
            lambda p: outgoing.at[p, pl.ds(0, CAP)],
            lambda p: back.at[p, pl.ds(0, CAP)],
            o_send,
            o_recv,
            d,
            away,
        )

    for copy in initial:
        weight_copy(copy, False).start()
    for d in range(1, EXPERTS):
        meta_copy(d, True).start()
    metas[me] = meta_ref[...]

    tokens_pad[TOK // 8 * 8 :, :] = jnp.zeros((256 - TOK // 8 * 8, D), jnp.bfloat16)
    tokens_pad[0:TOK, :] = tokens_ref[...]
    placing = slots_of(meta_ref[0:1, :], ROWS)
    scale = jnp.sum(placing * weight_ref[...], axis=1, keepdims=True)
    picked = jnp.dot(
        placing.astype(jnp.bfloat16), tokens_pad[...], preferred_element_type=jnp.float32
    ).astype(jnp.bfloat16)
    send[:, :, 0:D] = picked.reshape(EXPERTS, SLOT, D)
    send[:, :, D:WIDE] = (
        jnp.broadcast_to(scale, (ROWS, 128)).astype(jnp.bfloat16).reshape(EXPERTS, SLOT, 128)
    )
    for d in range(1, EXPERTS):
        token_copy(d, True).start()
    got[me, 0:CAP, :] = send[me, 0:CAP, :]

    def begin_tokens():
        for d in range(1, EXPERTS):
            token_copy(d, False).wait_recv()
        rows = got[:, :, 0:D].reshape(ROWS, D)
        normed[...] = layer_norm(rows, gain_ref[...]).astype(jnp.bfloat16)
        total[...] = jnp.zeros((ROWS, D), jnp.float32)

    def slab(k):
        zi = at_z(-k)

        @pl.loop(0, 2)
        def _(tile):
            part = pl.ds(pl.multiple_of(tile * 256, 256), 256)
            first = w[zi, :, 0:UNITS, :].reshape(NX * UNITS, D)
            second = w[zi, :, UNITS : 2 * UNITS, :].reshape(NX * UNITS, D)
            hidden = gelu(
                lax.dot_general(
                    normed[part, :],
                    first,
                    (((1,), (1,)), ((), ())),
                    preferred_element_type=jnp.float32,
                )
            ).astype(jnp.bfloat16)
            total[part, :] += jnp.dot(hidden, second, preferred_element_type=jnp.float32)

    begun = False
    arrived = set()
    done = set()
    for now, copy, nexts in order:
        weight_copy(copy, True).wait_recv()
        for c in nexts:
            weight_copy(c, False).start()
        arrived.add(copy)
        if not begun and now > TOKENS_AT:
            begin_tokens()
            begun = True
        if begun:
            for k in range(NZ):
                if k not in done and slabs[k] <= arrived:
                    slab(k)
                    done.add(k)

    rows = got[:, :, 0:D].reshape(ROWS, D).astype(jnp.float32)
    scaling = got[:, :, D:WIDE].reshape(ROWS, 128)[:, 0:1].astype(jnp.float32)
    merged = (rows + scaling * total[...]).astype(jnp.bfloat16)
    final_normed = layer_norm(merged, final_ref[...]).astype(jnp.bfloat16)
    embedded = jnp.dot(
        final_normed, embed_ref[...], preferred_element_type=jnp.float32
    ).astype(jnp.bfloat16)
    for d in range(1, EXPERTS):
        meta_copy(d, False).wait_recv()
    owners = metas[:, 5, :][:, 0:1]
    lane = lax.broadcasted_iota(jnp.int32, (EXPERTS, ROWS), 1)
    member = lax.broadcasted_iota(jnp.int32, (EXPERTS, ROWS), 0)
    owner_lane = jnp.sum(
        jnp.where(lax.div(lane, SLOT) == member, owners, 0), axis=0, keepdims=True
    )
    row_at = lax.broadcasted_iota(jnp.int32, (ROWS, ROWS), 0)
    lane_at = lax.broadcasted_iota(jnp.int32, (ROWS, ROWS), 1)
    target_row = owner_lane * SLOT + lax.rem(lane_at[0:1, :], SLOT)
    permute = (row_at == target_row).astype(jnp.float32).astype(jnp.bfloat16)
    outgoing[...] = (
        jnp.dot(permute, embedded, preferred_element_type=jnp.float32)
        .astype(jnp.bfloat16)
        .reshape(EXPERTS, SLOT, DD)
    )
    for d in range(1, EXPERTS):
        back_copy(d, True).start()
    back[me, 0:CAP, :] = outgoing[me, 0:CAP, :]
    own_meta = jnp.zeros((8, 256), jnp.int32)
    for s in range(EXPERTS):
        entry = metas[s]
        own_meta = own_meta + jnp.where(entry[5:6, :] == me, entry, 0)
    own_meta_ref[...] = own_meta
    table = jnp.transpose(slots_of(own_meta[0:1, :], ROWS)).astype(jnp.bfloat16)
    for d in range(1, EXPERTS):
        back_copy(d, False).wait_recv()
    rows_ref[...] = jnp.dot(
        table, back[...].reshape(ROWS, DD), preferred_element_type=jnp.float32
    ).astype(jnp.bfloat16)
    for copy in ids:
        weight_copy(copy, False).wait_send()
    for d in range(1, EXPERTS):
        meta_copy(d, True).wait_send()
        token_copy(d, True).wait_send()
        back_copy(d, True).wait_send()


def expert_stage(*operands):
    vmem = pl.BlockSpec(memory_space=pltpu.VMEM)
    hbm = pl.BlockSpec(memory_space=pl.ANY)
    count = len(build_plan()[3])
    dma = pltpu.SemaphoreType.DMA
    return pl.pallas_call(
        expert_kernel,
        out_shape=(
            jax.ShapeDtypeStruct((256, DD), jnp.bfloat16),
            jax.ShapeDtypeStruct((8, 256), jnp.int32),
        ),
        in_specs=[vmem, vmem, vmem, vmem, hbm, hbm, vmem, vmem],
        out_specs=(vmem, vmem),
        scratch_shapes=[
            pltpu.VMEM((NZ, NX, 2 * UNITS, D), jnp.bfloat16),
            pltpu.VMEM((256, D), jnp.bfloat16),
            pltpu.VMEM((EXPERTS, SLOT, WIDE), jnp.bfloat16),
            pltpu.VMEM((EXPERTS, SLOT, WIDE), jnp.bfloat16),
            pltpu.VMEM((EXPERTS, 8, 256), jnp.int32),
            pltpu.VMEM((ROWS, D), jnp.bfloat16),
            pltpu.VMEM((ROWS, D), jnp.float32),
            pltpu.VMEM((EXPERTS, SLOT, DD), jnp.bfloat16),
            pltpu.VMEM((EXPERTS, SLOT, DD), jnp.bfloat16),
            dma((2,)),
            dma((count,)),
            dma((count,)),
            dma((EXPERTS,)),
            dma((EXPERTS,)),
            dma((EXPERTS,)),
            dma((EXPERTS,)),
            dma((EXPERTS,)),
            dma((EXPERTS,)),
        ],
        compiler_params=pltpu.CompilerParams(
            collective_id=0, has_side_effects=True, vmem_limit_bytes=48 * 1024 * 1024
        ),
    )(*operands)


def per_device(
    tokens,
    route_weight,
    expert_ids,
    visible,
    owner_map,
    norm_gain,
    expert_in,
    expert_out,
    final_gain,
    embed_weight,
    mask_token,
    decoder_pos,
    decoder_gain,
    attention_in,
    attention_out,
):
    img_dev = visible.shape[0]
    meta = jnp.concatenate(
        [
            jnp.pad(expert_ids.reshape(1, TOK), ((0, 0), (0, 256 - TOK)), constant_values=-1),
            jnp.pad(visible, ((0, 0), (0, 256 - VIS))),
            jnp.broadcast_to(owner_map[0], (3, 256)),
        ],
        axis=0,
    )
    weight_row = jnp.pad(
        route_weight.astype(jnp.float32).reshape(1, TOK), ((0, 0), (0, 256 - TOK))
    )
    embedded, own_meta = expert_stage(
        tokens,
        weight_row,
        meta,
        norm_gain.reshape(1, D),
        expert_in,
        expert_out,
        final_gain.reshape(1, D),
        embed_weight,
    )
    source_visible = own_meta[1:5, 0:VIS]
    image_rows = embedded[0:TOK].reshape(img_dev, 1, VIS, DD)
    image_places = source_visible.reshape(img_dev, 1, VIS)

    def decode_image(operands):
        rows_one, places_one = operands
        position_hit = places_one[:, :, None] == jnp.arange(GRID, dtype=jnp.int32)[None, None, :]
        covered = jnp.any(position_hit, axis=1)
        placed = jnp.einsum(
            "ivg,ivd->igd",
            position_hit.astype(jnp.bfloat16),
            rows_one,
            preferred_element_type=jnp.float32,
        )
        canvas = jnp.where(
            covered[:, :, None], placed, mask_token.astype(jnp.float32)[None, None, :]
        )
        initial = canvas + decoder_pos.astype(jnp.float32)[None]
        dec_normed = layer_norm(initial, decoder_gain).astype(jnp.bfloat16)
        projected = jnp.dot(
            dec_normed.reshape(GRID, DD), attention_in, preferred_element_type=jnp.float32
        ).astype(jnp.bfloat16)
        projected = projected.reshape(1, GRID, 3, HEADS, HEAD_DIM)
        queries = projected[:, :, 0]
        key_rows = projected[:, :, 1]
        value_rows = projected[:, :, 2]
        scores = jnp.einsum(
            "iqhc,ikhc->ihqk", queries, key_rows, preferred_element_type=jnp.float32
        ) * HEAD_DIM ** (-0.5)
        highest = jnp.max(scores, axis=-1, keepdims=True)
        raised = jnp.exp(scores - highest)
        weights = (raised / jnp.sum(raised, axis=-1, keepdims=True)).astype(jnp.bfloat16)
        mixed = jnp.einsum(
            "ihqk,ikhc->iqhc", weights, value_rows, preferred_element_type=jnp.float32
        ).astype(jnp.bfloat16)
        update_out = jnp.dot(
            mixed.reshape(GRID, DD), attention_out, preferred_element_type=jnp.float32
        )
        return (initial + update_out.reshape(1, GRID, DD)).astype(jnp.bfloat16)

    decoded = lax.map(decode_image, (image_rows, image_places))
    return decoded.reshape(img_dev, GRID, DD)


def solution(mesh):
    return jax.shard_map(
        per_device,
        mesh=mesh,
        in_specs=(
            P(("dp", "expert"), None),
            P(("dp", "expert")),
            P(("dp", "expert"), None),
            P(("dp", "expert"), None),
            P(("dp", "expert")),
            P(),
            P("expert", "dp", None),
            P("expert", "dp", None),
            P(),
            P(),
            P(),
            P(),
            P(),
            P(),
            P(),
        ),
        out_specs=P(("dp", "expert"), None, None),
        check_vma=False,
    )
```

```python
import heapq

import jax
import jax.numpy as jnp
from jax import lax
from jax.experimental import pallas as pl
from jax.experimental.pallas import tpu as pltpu
from jax.sharding import PartitionSpec as P

D = 1024
HEADS = 16
HEAD_DIM = 32
DD = 512
GRID = 196
VIS = 49
TOK = 196
EXPERTS = 16
CAP = 24
SLOT = 32
ROWS = EXPERTS * SLOT
WIDE = D + 128
NX = 4
NZ = 8
UNITS = 64
PART = 48
EPSILON = 1e-06
TOKENS_AT = 20.0
IMAGES = 4
KEYS = 256
QUERIES = 208


def layer_norm(values, factor):
    values = values.astype(jnp.float32)
    centered = values - jnp.mean(values, axis=-1, keepdims=True)
    variance = jnp.mean(centered * centered, axis=-1, keepdims=True)
    return centered * lax.rsqrt(variance + EPSILON) * factor


def a2_max(j, way):
    return 4 if (way == 1) == (j == 0) else 3


def b1_max(way):
    return 4 if way == 1 else 3


def b2_max(k, way):
    return 2 if (way == 1) == (k % 2 == 0) else 1


def a_from(j):
    return {0: None, 1: ("a1", 0), 2: ("a1", 2), 3: ("a1", 1)}[j]


def z_step(k, longest):
    return (1, k) if k <= longest else (-1, NZ - k)


def build_plan():
    need = {("a1", 0): None, ("a1", 1): None, ("a1", 2): ("a1", 0)}
    for way in (1, -1):
        for t in range(1, b1_max(way) + 1):
            need[("b1", way, t)] = None if t == 1 else ("b1", way, t - 1)
    for k in range(NZ):
        way0, t0 = z_step(k, b1_max(1))
        for way in (1, -1):
            for t in range(1, b2_max(k, way) + 1):
                first = None if k == 0 else ("b1", way0, t0)
                need[("b2", k, way, t)] = first if t == 1 else ("b2", k, way, t - 1)
    for j in range(NX):
        for way in (1, -1):
            for t in range(1, a2_max(j, way) + 1):
                need[("a2", j, way, t)] = a_from(j) if t == 1 else ("a2", j, way, t - 1)

    def link(copy):
        if copy[0] == "a1":
            return ("x", -1 if copy[1] == 1 else 1)
        if copy[0] == "b2":
            return ("x", copy[2])
        return ("z", copy[2] if copy[0] == "a2" else copy[1])

    free = {}
    arrivals = []

    def push(copy, now):
        took = 2.1 if copy[0][0] == "a" else 3.5
        begin = max(now, free.get(link(copy), 0.0))
        free[link(copy)] = begin + took
        heapq.heappush(arrivals, (begin + took + 1.5, len(order) + len(arrivals), copy))

    order = []
    initial = [c for c in need if need[c] is None]
    for copy in initial:
        push(copy, 0.0)
    while arrivals:
        now, _, copy = heapq.heappop(arrivals)
        nexts = [c for c in need if need[c] == copy]
        order.append((now, copy, nexts))
        for c in nexts:
            push(c, now)
    slabs = []
    for k in range(NZ):
        wants = set(("b2", k, way, t) for way in (1, -1) for t in range(1, b2_max(k, way) + 1))
        if k == 0:
            wants |= {("a1", 0), ("a1", 1), ("a1", 2)}
        else:
            wants.add(("b1",) + z_step(k, b1_max(1)))
            for j in range(NX):
                wants.add(("a2", j) + z_step(k, a2_max(j, 1)))
        slabs.append(wants)
    ids = {c: i for i, c in enumerate(need)}
    return initial, order, slabs, ids


def slots_of(ids_row, rows):
    lane = ids_row.shape[1]
    expert = lax.broadcasted_iota(jnp.int32, (EXPERTS, lane), 0)
    onehot = (expert == ids_row).astype(jnp.float32)
    before = (
        lax.broadcasted_iota(jnp.int32, (lane, lane), 0)
        < lax.broadcasted_iota(jnp.int32, (lane, lane), 1)
    ).astype(jnp.bfloat16)
    count = jnp.dot(onehot.astype(jnp.bfloat16), before, preferred_element_type=jnp.float32)
    earlier = jnp.sum(count * onehot, axis=0, keepdims=True).astype(jnp.int32)
    slot = ids_row * SLOT + earlier
    return (lax.broadcasted_iota(jnp.int32, (rows, lane), 0) == slot).astype(jnp.float32)


def gelu(value):
    inner = 0.7978845608028654 * (value + 0.044715 * (value * value * value))
    return 0.5 * value * (1.0 + jnp.tanh(inner))


def expert_kernel(
    tokens_hbm,
    weight_ref,
    ids_ref,
    visible_ref,
    owner_ref,
    gain_hbm,
    in_ref,
    out_ref,
    final_hbm,
    embed_hbm,
    rows_ref,
    own_meta_ref,
    tokens_ref,
    gain_ref,
    final_ref,
    embed_ref,
    meta_ref,
    w,
    tokens_pad,
    send,
    got,
    metas,
    normed,
    total,
    outgoing,
    back,
    local_sems,
    w_send,
    w_recv,
    t_send,
    t_recv,
    m_send,
    m_recv,
    o_send,
    o_recv,
):
    initial, order, slabs, ids = build_plan()
    dp = lax.axis_index("dp")
    me = lax.axis_index("expert")
    z, x = lax.div(dp, NX), lax.rem(dp, NX)

    def at_z(step):
        return lax.rem(z + (step + NZ), NZ)

    def at_x(step):
        return lax.rem(x + (step + NX), NX)

    own_in = pltpu.make_async_copy(in_ref.at[0], w.at[z, x, pl.ds(0, UNITS)], local_sems.at[0])
    own_out = pltpu.make_async_copy(
        out_ref.at[0], w.at[z, x, pl.ds(UNITS, UNITS)], local_sems.at[1]
    )
    own_in.start()
    own_out.start()
    fetches = [
        pltpu.make_async_copy(src, dst, local_sems.at[2 + n])
        for n, (src, dst) in enumerate(
            (
                (tokens_hbm, tokens_ref),
                (gain_hbm, gain_ref),
                (final_hbm, final_ref),
                (embed_hbm, embed_ref),
            )
        )
    ]
    for fetch in fetches:
        fetch.start()
    barrier = pltpu.get_barrier_semaphore()
    for near in (
        at_z(0) * NX + at_x(1),
        at_z(0) * NX + at_x(-1),
        at_z(1) * NX + at_x(0),
        at_z(-1) * NX + at_x(0),
    ):
        pl.semaphore_signal(
            barrier, inc=1, device_id={"dp": near}, device_id_type=pl.DeviceIdType.MESH
        )
    for d in range(1, EXPERTS):
        pl.semaphore_signal(
            barrier,
            inc=1,
            device_id={"expert": lax.rem(me + d, EXPERTS)},
            device_id_type=pl.DeviceIdType.MESH,
        )
    got[:, CAP:SLOT, :] = jnp.zeros((EXPERTS, SLOT - CAP, WIDE), jnp.bfloat16)
    back[:, CAP:SLOT, :] = jnp.zeros((EXPERTS, SLOT - CAP, DD), jnp.bfloat16)
    pad = jnp.full((1, 256 - TOK), -1, jnp.int32)
    meta_ref[0:1, :] = jnp.concatenate([ids_ref[...], pad], axis=1)
    for i in range(IMAGES):
        parts = [visible_ref[i : i + 1, :], jnp.full((1, 256 - VIS * (i + 1)), -1, jnp.int32)]
        if i > 0:
            parts = [jnp.full((1, VIS * i), -1, jnp.int32)] + parts
        meta_ref[i + 1 : i + 2, :] = jnp.concatenate(parts, axis=1)
    meta_ref[5:8, :] = jnp.full((3, 256), owner_ref[0], jnp.int32)
    own_in.wait()
    own_out.wait()
    pl.semaphore_wait(barrier, 4 + EXPERTS - 1)

    def weight_copy(copy, arriving):
        kind = copy[0]
        shift = 1 if arriving else 0
        if kind == "a1":
            step = -1 if copy[1] == 1 else 1
            first = 1 if copy[1] == 2 else 0
            zi, xi = z, at_x(-step * (first + shift))
            target = at_z(0) * NX + at_x(step)
        elif kind == "b2":
            _, k, step, t = copy
            zi, xi = at_z(-k), at_x(-step * (t - 1 + shift))
            target = at_z(0) * NX + at_x(step)
        else:
            step, t = copy[-2:]
            j = copy[1] if kind == "a2" else 0
            zi, xi = at_z(-step * (t - 1 + shift)), at_x(-j)
            target = at_z(step) * NX + at_x(0)
        part = pl.ds(0, PART) if kind[0] == "a" else pl.ds(PART, 2 * UNITS - PART)
        block = w.at[zi, xi, part]
        return pltpu.make_async_remote_copy(
            src_ref=block,
            dst_ref=block,
            send_sem=w_send.at[ids[copy]],
            recv_sem=w_recv.at[ids[copy]],
            device_id={"dp": target},
            device_id_type=pl.DeviceIdType.MESH,
        )

    def exchange(src, dst, send_sem, recv_sem, d, away):
        peer = lax.rem(me + d, EXPERTS)
        from_peer = lax.rem(me + (EXPERTS - d), EXPERTS)
        return pltpu.make_async_remote_copy(
            src_ref=src(peer),
            dst_ref=dst(me if away else from_peer),
            send_sem=send_sem.at[d],
            recv_sem=recv_sem.at[d],
            device_id={"expert": peer},
            device_id_type=pl.DeviceIdType.MESH,
        )

    def meta_copy(d, away):
        return exchange(lambda p: meta_ref, lambda p: metas.at[p], m_send, m_recv, d, away)

    def token_copy(d, away):
        return exchange(
            lambda p: send.at[p, pl.ds(0, CAP)],
            lambda p: got.at[p, pl.ds(0, CAP)],
            t_send,
            t_recv,
            d,
            away,
        )

    def back_copy(d, away):
        return exchange(
            lambda p: outgoing.at[p, pl.ds(0, CAP)],
            lambda p: back.at[p, pl.ds(0, CAP)],
            o_send,
            o_recv,
            d,
            away,
        )

    for copy in initial:
        weight_copy(copy, False).start()
    for d in range(1, EXPERTS):
        meta_copy(d, True).start()
    metas[me] = meta_ref[...]

    for fetch in fetches:
        fetch.wait()
    tokens_pad[TOK // 8 * 8 :, :] = jnp.zeros((256 - TOK // 8 * 8, D), jnp.bfloat16)
    tokens_pad[0:TOK, :] = tokens_ref[...]
    placing = slots_of(meta_ref[0:1, :], ROWS)
    weight_row = jnp.concatenate(
        [weight_ref[...].astype(jnp.float32), jnp.zeros((1, 256 - TOK), jnp.float32)], axis=1
    )
    scale = jnp.sum(placing * weight_row, axis=1, keepdims=True)
    picked = jnp.dot(
        placing.astype(jnp.bfloat16), tokens_pad[...], preferred_element_type=jnp.float32
    ).astype(jnp.bfloat16)
    send[:, :, 0:D] = picked.reshape(EXPERTS, SLOT, D)
    send[:, :, D:WIDE] = (
        jnp.broadcast_to(scale, (ROWS, 128)).astype(jnp.bfloat16).reshape(EXPERTS, SLOT, 128)
    )
    for d in range(1, EXPERTS):
        token_copy(d, True).start()
    got[me, 0:CAP, :] = send[me, 0:CAP, :]

    def begin_tokens():
        for d in range(1, EXPERTS):
            token_copy(d, False).wait_recv()
        rows = got[:, :, 0:D].reshape(ROWS, D)
        normed[...] = layer_norm(rows, gain_ref[...]).astype(jnp.bfloat16)
        total[...] = jnp.zeros((ROWS, D), jnp.float32)

    def slab(k):
        zi = at_z(-k)

        @pl.loop(0, 2)
        def _(tile):
            part = pl.ds(pl.multiple_of(tile * 256, 256), 256)
            first = w[zi, :, 0:UNITS, :].reshape(NX * UNITS, D)
            second = w[zi, :, UNITS : 2 * UNITS, :].reshape(NX * UNITS, D)
            hidden = gelu(
                lax.dot_general(
                    normed[part, :],
                    first,
                    (((1,), (1,)), ((), ())),
                    preferred_element_type=jnp.float32,
                )
            ).astype(jnp.bfloat16)
            total[part, :] += jnp.dot(hidden, second, preferred_element_type=jnp.float32)

    begun = False
    arrived = set()
    done = set()
    for now, copy, nexts in order:
        weight_copy(copy, True).wait_recv()
        for c in nexts:
            weight_copy(c, False).start()
        arrived.add(copy)
        if not begun and now > TOKENS_AT:
            begin_tokens()
            begun = True
        if begun:
            for k in range(NZ):
                if k not in done and slabs[k] <= arrived:
                    slab(k)
                    done.add(k)

    rows = got[:, :, 0:D].reshape(ROWS, D).astype(jnp.float32)
    scaling = got[:, :, D:WIDE].reshape(ROWS, 128)[:, 0:1].astype(jnp.float32)
    merged = (rows + scaling * total[...]).astype(jnp.bfloat16)
    final_normed = layer_norm(merged, final_ref[...]).astype(jnp.bfloat16)
    embedded = jnp.dot(
        final_normed, embed_ref[...], preferred_element_type=jnp.float32
    ).astype(jnp.bfloat16)
    for d in range(1, EXPERTS):
        meta_copy(d, False).wait_recv()
    owners = metas[:, 5, :][:, 0:1]
    lane = lax.broadcasted_iota(jnp.int32, (EXPERTS, ROWS), 1)
    member = lax.broadcasted_iota(jnp.int32, (EXPERTS, ROWS), 0)
    owner_lane = jnp.sum(
        jnp.where(lax.div(lane, SLOT) == member, owners, 0), axis=0, keepdims=True
    )
    row_at = lax.broadcasted_iota(jnp.int32, (ROWS, ROWS), 0)
    lane_at = lax.broadcasted_iota(jnp.int32, (ROWS, ROWS), 1)
    target_row = owner_lane * SLOT + lax.rem(lane_at[0:1, :], SLOT)
    permute = (row_at == target_row).astype(jnp.float32).astype(jnp.bfloat16)
    outgoing[...] = (
        jnp.dot(permute, embedded, preferred_element_type=jnp.float32)
        .astype(jnp.bfloat16)
        .reshape(EXPERTS, SLOT, DD)
    )
    for d in range(1, EXPERTS):
        back_copy(d, True).start()
    back[me, 0:CAP, :] = outgoing[me, 0:CAP, :]
    own_meta = jnp.zeros((8, 256), jnp.int32)
    for s in range(EXPERTS):
        entry = metas[s]
        own_meta = own_meta + jnp.where(entry[5:6, :] == me, entry, 0)
    own_meta_ref[...] = own_meta
    table = jnp.transpose(slots_of(own_meta[0:1, :], ROWS)).astype(jnp.bfloat16)
    for d in range(1, EXPERTS):
        back_copy(d, False).wait_recv()
    rows_ref[...] = jnp.dot(
        table, back[...].reshape(ROWS, DD), preferred_element_type=jnp.float32
    ).astype(jnp.bfloat16)
    for copy in ids:
        weight_copy(copy, False).wait_send()
    for d in range(1, EXPERTS):
        meta_copy(d, True).wait_send()
        token_copy(d, True).wait_send()
        back_copy(d, True).wait_send()


def expert_stage(*operands):
    vmem = pl.BlockSpec(memory_space=pltpu.VMEM)
    hbm = pl.BlockSpec(memory_space=pltpu.HBM)
    smem = pl.BlockSpec(memory_space=pltpu.SMEM)
    count = len(build_plan()[3])
    dma = pltpu.SemaphoreType.DMA
    return pl.pallas_call(
        expert_kernel,
        out_shape=(
            jax.ShapeDtypeStruct((256, DD), jnp.bfloat16),
            jax.ShapeDtypeStruct((8, 256), jnp.int32),
        ),
        in_specs=[hbm, vmem, vmem, vmem, smem, hbm, hbm, hbm, hbm, hbm],
        out_specs=(vmem, vmem),
        scratch_shapes=[
            pltpu.VMEM((TOK, D), jnp.bfloat16),
            pltpu.VMEM((1, D), jnp.float32),
            pltpu.VMEM((1, D), jnp.float32),
            pltpu.VMEM((D, DD), jnp.bfloat16),
            pltpu.VMEM((8, 256), jnp.int32),
            pltpu.VMEM((NZ, NX, 2 * UNITS, D), jnp.bfloat16),
            pltpu.VMEM((256, D), jnp.bfloat16),
            pltpu.VMEM((EXPERTS, SLOT, WIDE), jnp.bfloat16),
            pltpu.VMEM((EXPERTS, SLOT, WIDE), jnp.bfloat16),
            pltpu.VMEM((EXPERTS, 8, 256), jnp.int32),
            pltpu.VMEM((ROWS, D), jnp.bfloat16),
            pltpu.VMEM((ROWS, D), jnp.float32),
            pltpu.VMEM((EXPERTS, SLOT, DD), jnp.bfloat16),
            pltpu.VMEM((EXPERTS, SLOT, DD), jnp.bfloat16),
            dma((6,)),
            dma((count,)),
            dma((count,)),
            dma((EXPERTS,)),
            dma((EXPERTS,)),
            dma((EXPERTS,)),
            dma((EXPERTS,)),
            dma((EXPERTS,)),
            dma((EXPERTS,)),
        ],
        compiler_params=pltpu.CompilerParams(
            collective_id=0, has_side_effects=True, vmem_limit_bytes=67043328
        ),
    )(*operands)


def decoder_kernel(
    rows_ref, meta_ref, mask_ref, pos_ref, gain_ref, in_ref, out_w_ref, out_ref, start, projected, mixed
):
    start[:, GRID // 8 * 8 :, :] = jnp.zeros((IMAGES, KEYS - GRID // 8 * 8, DD), jnp.float32)
    mask_row = mask_ref[...].astype(jnp.float32)
    position = lax.broadcasted_iota(jnp.int32, (GRID, 256), 0)

    @pl.loop(0, IMAGES)
    def _(i):
        hit = (position == meta_ref[pl.ds(i + 1, 1), :]).astype(jnp.float32)
        covered = jnp.sum(hit, axis=1, keepdims=True)
        placed = jnp.dot(
            hit.astype(jnp.bfloat16), rows_ref[...], preferred_element_type=jnp.float32
        )
        initial = jnp.where(covered > 0.5, placed, mask_row) + pos_ref[...].astype(jnp.float32)
        start[i, 0:GRID, :] = initial
        dec_normed = layer_norm(start[i], gain_ref[...]).astype(jnp.bfloat16)
        projected[i] = jnp.dot(
            dec_normed, in_ref[...], preferred_element_type=jnp.float32
        ).astype(jnp.bfloat16)

    lane = lax.broadcasted_iota(jnp.int32, (QUERIES, KEYS), 1)
    head_lane = lax.div(lax.broadcasted_iota(jnp.int32, (1, 128), 1), HEAD_DIM)
    own_lanes = [(head_lane == h).astype(jnp.float32).astype(jnp.bfloat16) for h in range(4)]
    exponent = HEAD_DIM ** (-0.5) * 1.4426950408889634

    @pl.loop(0, IMAGES)
    def _(i):
        for g in range(HEADS // 4):
            queries = projected[i, 0:QUERIES, g * 128 : (g + 1) * 128]
            keys = projected[i, :, DD + g * 128 : DD + (g + 1) * 128]
            values = projected[i, :, 2 * DD + g * 128 : 2 * DD + (g + 1) * 128]
            total = jnp.zeros((QUERIES, 128), jnp.float32)
            for h in range(4):
                scores = lax.dot_general(
                    queries,
                    keys * own_lanes[h],
                    (((1,), (1,)), ((), ())),
                    preferred_element_type=jnp.float32,
                )
                scores = jnp.where(lane < GRID, scores, -jnp.inf)
                highest = jnp.max(scores, axis=1, keepdims=True)
                raised = jnp.exp2((scores - highest) * exponent)
                share = 1.0 / jnp.sum(raised, axis=1, keepdims=True)
                weights = (raised * share).astype(jnp.bfloat16)
                total = total + jnp.dot(
                    weights, values * own_lanes[h], preferred_element_type=jnp.float32
                )
            mixed[:, g * 128 : (g + 1) * 128] = total.astype(jnp.bfloat16)
        update = jnp.dot(mixed[...], out_w_ref[...], preferred_element_type=jnp.float32)
        out_ref[i] = (start[i, 0:GRID, :] + update[0:GRID]).astype(jnp.bfloat16)


def decoder_stage(*operands):
    vmem = pl.BlockSpec(memory_space=pltpu.VMEM)
    return pl.pallas_call(
        decoder_kernel,
        out_shape=jax.ShapeDtypeStruct((IMAGES, GRID, DD), jnp.bfloat16),
        in_specs=[vmem] * 7,
        out_specs=vmem,
        scratch_shapes=[
            pltpu.VMEM((IMAGES, KEYS, DD), jnp.float32),
            pltpu.VMEM((IMAGES, KEYS, 3 * DD), jnp.bfloat16),
            pltpu.VMEM((QUERIES, DD), jnp.bfloat16),
        ],
        compiler_params=pltpu.CompilerParams(vmem_limit_bytes=67043328),
    )(*operands)


def per_device(
    tokens,
    route_weight,
    expert_ids,
    visible,
    owner_map,
    norm_gain,
    expert_in,
    expert_out,
    final_gain,
    embed_weight,
    mask_token,
    decoder_pos,
    decoder_gain,
    attention_in,
    attention_out,
):
    embedded, own_meta = expert_stage(
        tokens,
        route_weight.reshape(1, TOK),
        expert_ids.reshape(1, TOK),
        visible,
        owner_map,
        norm_gain.reshape(1, D),
        expert_in,
        expert_out,
        final_gain.reshape(1, D),
        embed_weight,
    )
    return decoder_stage(
        embedded,
        own_meta,
        mask_token.reshape(1, DD),
        decoder_pos,
        decoder_gain.reshape(1, DD),
        attention_in,
        attention_out,
    )


def solution(mesh):
    return jax.shard_map(
        per_device,
        mesh=mesh,
        in_specs=(
            P(("dp", "expert"), None),
            P(("dp", "expert")),
            P(("dp", "expert"), None),
            P(("dp", "expert"), None),
            P(("dp", "expert")),
            P(),
            P("expert", "dp", None),
            P("expert", "dp", None),
            P(),
            P(),
            P(),
            P(),
            P(),
            P(),
            P(),
        ),
        out_specs=P(("dp", "expert"), None, None),
        check_vma=False,
    )
```

```python
import heapq

import jax
import jax.numpy as jnp
from jax import lax
from jax.experimental import pallas as pl
from jax.experimental.pallas import tpu as pltpu
from jax.sharding import PartitionSpec as P

D = 1024
HEADS = 16
HEAD_DIM = 32
DD = 512
GRID = 196
VIS = 49
TOK = 196
EXPERTS = 16
CAP = 24
SLOT = 32
ROWS = EXPERTS * SLOT
WIDE = D + 128
NX = 4
NZ = 8
UNITS = 64
PART = 48
EPSILON = 1e-06
TOKENS_AT = 20.0
IMAGES = 4
LANES = 256
KEYS = 208
FULL = 192


def layer_norm(values, factor):
    values = values.astype(jnp.float32)
    centered = values - jnp.mean(values, axis=-1, keepdims=True)
    variance = jnp.mean(centered * centered, axis=-1, keepdims=True)
    return centered * lax.rsqrt(variance + EPSILON) * factor


def a2_max(j, way):
    return 4 if (way == 1) == (j == 0) else 3


def b1_max(way):
    return 4 if way == 1 else 3


def b2_max(k, way):
    return 2 if (way == 1) == (k % 2 == 0) else 1


def a_from(j):
    return {0: None, 1: ("a1", 0), 2: ("a1", 2), 3: ("a1", 1)}[j]


def z_step(k, longest):
    return (1, k) if k <= longest else (-1, NZ - k)


def build_plan():
    need = {("a1", 0): None, ("a1", 1): None, ("a1", 2): ("a1", 0)}
    for way in (1, -1):
        for t in range(1, b1_max(way) + 1):
            need[("b1", way, t)] = None if t == 1 else ("b1", way, t - 1)
    for k in range(NZ):
        way0, t0 = z_step(k, b1_max(1))
        for way in (1, -1):
            for t in range(1, b2_max(k, way) + 1):
                first = None if k == 0 else ("b1", way0, t0)
                need[("b2", k, way, t)] = first if t == 1 else ("b2", k, way, t - 1)
    for j in range(NX):
        for way in (1, -1):
            for t in range(1, a2_max(j, way) + 1):
                need[("a2", j, way, t)] = a_from(j) if t == 1 else ("a2", j, way, t - 1)

    def link(copy):
        if copy[0] == "a1":
            return ("x", -1 if copy[1] == 1 else 1)
        if copy[0] == "b2":
            return ("x", copy[2])
        return ("z", copy[2] if copy[0] == "a2" else copy[1])

    free = {}
    arrivals = []

    def push(copy, now):
        took = 2.1 if copy[0][0] == "a" else 3.5
        begin = max(now, free.get(link(copy), 0.0))
        free[link(copy)] = begin + took
        heapq.heappush(arrivals, (begin + took + 1.5, len(order) + len(arrivals), copy))

    order = []
    initial = [c for c in need if need[c] is None]
    for copy in initial:
        push(copy, 0.0)
    while arrivals:
        now, _, copy = heapq.heappop(arrivals)
        nexts = [c for c in need if need[c] == copy]
        order.append((now, copy, nexts))
        for c in nexts:
            push(c, now)
    slabs = []
    for k in range(NZ):
        wants = set(("b2", k, way, t) for way in (1, -1) for t in range(1, b2_max(k, way) + 1))
        if k == 0:
            wants |= {("a1", 0), ("a1", 1), ("a1", 2)}
        else:
            wants.add(("b1",) + z_step(k, b1_max(1)))
            for j in range(NX):
                wants.add(("a2", j) + z_step(k, a2_max(j, 1)))
        slabs.append(wants)
    ids = {c: i for i, c in enumerate(need)}
    return initial, order, slabs, ids


def slots_of(ids_row, rows):
    lane = ids_row.shape[1]
    expert = lax.broadcasted_iota(jnp.int32, (EXPERTS, lane), 0)
    onehot = (expert == ids_row).astype(jnp.float32)
    before = (
        lax.broadcasted_iota(jnp.int32, (lane, lane), 0)
        < lax.broadcasted_iota(jnp.int32, (lane, lane), 1)
    ).astype(jnp.bfloat16)
    count = jnp.dot(onehot.astype(jnp.bfloat16), before, preferred_element_type=jnp.float32)
    earlier = jnp.sum(count * onehot, axis=0, keepdims=True).astype(jnp.int32)
    slot = ids_row * SLOT + earlier
    return (lax.broadcasted_iota(jnp.int32, (rows, lane), 0) == slot).astype(jnp.float32)


def gelu(value):
    inner = 0.7978845608028654 * (value + 0.044715 * (value * value * value))
    return 0.5 * value * (1.0 + jnp.tanh(inner))


def expert_kernel(
    tokens_hbm,
    weight_ref,
    ids_ref,
    visible_ref,
    owner_ref,
    gain_hbm,
    in_ref,
    out_ref,
    final_hbm,
    embed_hbm,
    rows_ref,
    own_meta_ref,
    tokens_ref,
    gain_ref,
    final_ref,
    embed_ref,
    meta_ref,
    w,
    tokens_pad,
    send,
    got,
    metas,
    normed,
    total,
    outgoing,
    back,
    local_sems,
    w_send,
    w_recv,
    t_send,
    t_recv,
    m_send,
    m_recv,
    o_send,
    o_recv,
):
    initial, order, slabs, ids = build_plan()
    dp = lax.axis_index("dp")
    me = lax.axis_index("expert")
    z, x = lax.div(dp, NX), lax.rem(dp, NX)

    def at_z(step):
        return lax.rem(z + (step + NZ), NZ)

    def at_x(step):
        return lax.rem(x + (step + NX), NX)

    own_in = pltpu.make_async_copy(in_ref.at[0], w.at[z, x, pl.ds(0, UNITS)], local_sems.at[0])
    own_out = pltpu.make_async_copy(
        out_ref.at[0], w.at[z, x, pl.ds(UNITS, UNITS)], local_sems.at[1]
    )
    own_in.start()
    own_out.start()
    fetches = [
        pltpu.make_async_copy(src, dst, local_sems.at[2 + n])
        for n, (src, dst) in enumerate(
            (
                (tokens_hbm, tokens_ref),
                (gain_hbm, gain_ref),
                (final_hbm, final_ref),
                (embed_hbm, embed_ref),
            )
        )
    ]
    for fetch in fetches:
        fetch.start()
    barrier = pltpu.get_barrier_semaphore()
    for near in (
        at_z(0) * NX + at_x(1),
        at_z(0) * NX + at_x(-1),
        at_z(1) * NX + at_x(0),
        at_z(-1) * NX + at_x(0),
    ):
        pl.semaphore_signal(
            barrier, inc=1, device_id={"dp": near}, device_id_type=pl.DeviceIdType.MESH
        )
    for d in range(1, EXPERTS):
        pl.semaphore_signal(
            barrier,
            inc=1,
            device_id={"expert": lax.rem(me + d, EXPERTS)},
            device_id_type=pl.DeviceIdType.MESH,
        )
    got[:, CAP:SLOT, :] = jnp.zeros((EXPERTS, SLOT - CAP, WIDE), jnp.bfloat16)
    back[:, CAP:SLOT, :] = jnp.zeros((EXPERTS, SLOT - CAP, DD), jnp.bfloat16)
    pad = jnp.full((1, 256 - TOK), -1, jnp.int32)
    meta_ref[0:1, :] = jnp.concatenate([ids_ref[...], pad], axis=1)
    for i in range(IMAGES):
        parts = [visible_ref[i : i + 1, :], jnp.full((1, 256 - VIS * (i + 1)), -1, jnp.int32)]
        if i > 0:
            parts = [jnp.full((1, VIS * i), -1, jnp.int32)] + parts
        meta_ref[i + 1 : i + 2, :] = jnp.concatenate(parts, axis=1)
    meta_ref[5:8, :] = jnp.full((3, 256), owner_ref[0], jnp.int32)
    own_in.wait()
    own_out.wait()
    pl.semaphore_wait(barrier, 4 + EXPERTS - 1)

    def weight_copy(copy, arriving):
        kind = copy[0]
        shift = 1 if arriving else 0
        if kind == "a1":
            step = -1 if copy[1] == 1 else 1
            first = 1 if copy[1] == 2 else 0
            zi, xi = z, at_x(-step * (first + shift))
            target = at_z(0) * NX + at_x(step)
        elif kind == "b2":
            _, k, step, t = copy
            zi, xi = at_z(-k), at_x(-step * (t - 1 + shift))
            target = at_z(0) * NX + at_x(step)
        else:
            step, t = copy[-2:]
            j = copy[1] if kind == "a2" else 0
            zi, xi = at_z(-step * (t - 1 + shift)), at_x(-j)
            target = at_z(step) * NX + at_x(0)
        part = pl.ds(0, PART) if kind[0] == "a" else pl.ds(PART, 2 * UNITS - PART)
        block = w.at[zi, xi, part]
        return pltpu.make_async_remote_copy(
            src_ref=block,
            dst_ref=block,
            send_sem=w_send.at[ids[copy]],
            recv_sem=w_recv.at[ids[copy]],
            device_id={"dp": target},
            device_id_type=pl.DeviceIdType.MESH,
        )

    def exchange(src, dst, send_sem, recv_sem, d, away):
        peer = lax.rem(me + d, EXPERTS)
        from_peer = lax.rem(me + (EXPERTS - d), EXPERTS)
        return pltpu.make_async_remote_copy(
            src_ref=src(peer),
            dst_ref=dst(me if away else from_peer),
            send_sem=send_sem.at[d],
            recv_sem=recv_sem.at[d],
            device_id={"expert": peer},
            device_id_type=pl.DeviceIdType.MESH,
        )

    def meta_copy(d, away):
        return exchange(lambda p: meta_ref, lambda p: metas.at[p], m_send, m_recv, d, away)

    def token_copy(d, away):
        return exchange(
            lambda p: send.at[p, pl.ds(0, CAP)],
            lambda p: got.at[p, pl.ds(0, CAP)],
            t_send,
            t_recv,
            d,
            away,
        )

    def back_copy(d, away):
        return exchange(
            lambda p: outgoing.at[p, pl.ds(0, CAP)],
            lambda p: back.at[p, pl.ds(0, CAP)],
            o_send,
            o_recv,
            d,
            away,
        )

    for copy in initial:
        weight_copy(copy, False).start()
    for d in range(1, EXPERTS):
        meta_copy(d, True).start()
    metas[me] = meta_ref[...]

    for fetch in fetches:
        fetch.wait()
    tokens_pad[TOK // 8 * 8 :, :] = jnp.zeros((256 - TOK // 8 * 8, D), jnp.bfloat16)
    tokens_pad[0:TOK, :] = tokens_ref[...]
    placing = slots_of(meta_ref[0:1, :], ROWS)
    weight_row = jnp.concatenate(
        [weight_ref[...].astype(jnp.float32).reshape(1, TOK), jnp.zeros((1, 256 - TOK), jnp.float32)], axis=1
    )
    scale = jnp.sum(placing * weight_row, axis=1, keepdims=True)
    picked = jnp.dot(
        placing.astype(jnp.bfloat16), tokens_pad[...], preferred_element_type=jnp.float32
    ).astype(jnp.bfloat16)
    send[:, :, 0:D] = picked.reshape(EXPERTS, SLOT, D)
    send[:, :, D:WIDE] = (
        jnp.broadcast_to(scale, (ROWS, 128)).astype(jnp.bfloat16).reshape(EXPERTS, SLOT, 128)
    )
    for d in range(1, EXPERTS):
        token_copy(d, True).start()
    got[me, 0:CAP, :] = send[me, 0:CAP, :]

    def begin_tokens():
        for d in range(1, EXPERTS):
            token_copy(d, False).wait_recv()
        rows = got[:, :, 0:D].reshape(ROWS, D)
        normed[...] = layer_norm(rows, gain_ref[...]).astype(jnp.bfloat16)
        total[...] = jnp.zeros((ROWS, D), jnp.float32)

    def slab(k):
        zi = at_z(-k)

        @pl.loop(0, 2)
        def _(tile):
            part = pl.ds(pl.multiple_of(tile * 256, 256), 256)
            first = w[zi, :, 0:UNITS, :].reshape(NX * UNITS, D)
            second = w[zi, :, UNITS : 2 * UNITS, :].reshape(NX * UNITS, D)
            hidden = gelu(
                lax.dot_general(
                    normed[part, :],
                    first,
                    (((1,), (1,)), ((), ())),
                    preferred_element_type=jnp.float32,
                )
            ).astype(jnp.bfloat16)
            total[part, :] += jnp.dot(hidden, second, preferred_element_type=jnp.float32)

    begun = False
    arrived = set()
    done = set()
    for now, copy, nexts in order:
        weight_copy(copy, True).wait_recv()
        for c in nexts:
            weight_copy(c, False).start()
        arrived.add(copy)
        if not begun and now > TOKENS_AT:
            begin_tokens()
            begun = True
        if begun:
            for k in range(NZ):
                if k not in done and slabs[k] <= arrived:
                    slab(k)
                    done.add(k)

    rows = got[:, :, 0:D].reshape(ROWS, D).astype(jnp.float32)
    scaling = got[:, :, D:WIDE].reshape(ROWS, 128)[:, 0:1].astype(jnp.float32)
    merged = (rows + scaling * total[...]).astype(jnp.bfloat16)
    final_normed = layer_norm(merged, final_ref[...]).astype(jnp.bfloat16)
    embedded = jnp.dot(
        final_normed, embed_ref[...], preferred_element_type=jnp.float32
    ).astype(jnp.bfloat16)
    for d in range(1, EXPERTS):
        meta_copy(d, False).wait_recv()
    owners = metas[:, 5, :][:, 0:1]
    lane = lax.broadcasted_iota(jnp.int32, (EXPERTS, ROWS), 1)
    member = lax.broadcasted_iota(jnp.int32, (EXPERTS, ROWS), 0)
    owner_lane = jnp.sum(
        jnp.where(lax.div(lane, SLOT) == member, owners, 0), axis=0, keepdims=True
    )
    row_at = lax.broadcasted_iota(jnp.int32, (ROWS, ROWS), 0)
    lane_at = lax.broadcasted_iota(jnp.int32, (ROWS, ROWS), 1)
    target_row = owner_lane * SLOT + lax.rem(lane_at[0:1, :], SLOT)
    permute = (row_at == target_row).astype(jnp.float32).astype(jnp.bfloat16)
    outgoing[...] = (
        jnp.dot(permute, embedded, preferred_element_type=jnp.float32)
        .astype(jnp.bfloat16)
        .reshape(EXPERTS, SLOT, DD)
    )
    for d in range(1, EXPERTS):
        back_copy(d, True).start()
    back[me, 0:CAP, :] = outgoing[me, 0:CAP, :]
    own_meta = jnp.zeros((8, 256), jnp.int32)
    for s in range(EXPERTS):
        entry = metas[s]
        own_meta = own_meta + jnp.where(entry[5:6, :] == me, entry, 0)
    own_meta_ref[...] = own_meta
    table = jnp.transpose(slots_of(own_meta[0:1, :], ROWS)).astype(jnp.bfloat16)
    for d in range(1, EXPERTS):
        back_copy(d, False).wait_recv()
    rows_ref[...] = jnp.dot(
        table, back[...].reshape(ROWS, DD), preferred_element_type=jnp.float32
    ).astype(jnp.bfloat16)
    for copy in ids:
        weight_copy(copy, False).wait_send()
    for d in range(1, EXPERTS):
        meta_copy(d, True).wait_send()
        token_copy(d, True).wait_send()
        back_copy(d, True).wait_send()


def expert_stage(*operands):
    vmem = pl.BlockSpec(memory_space=pltpu.VMEM)
    hbm = pl.BlockSpec(memory_space=pltpu.HBM)
    smem = pl.BlockSpec(memory_space=pltpu.SMEM)
    count = len(build_plan()[3])
    dma = pltpu.SemaphoreType.DMA
    return pl.pallas_call(
        expert_kernel,
        out_shape=(
            jax.ShapeDtypeStruct((256, DD), jnp.bfloat16),
            jax.ShapeDtypeStruct((8, 256), jnp.int32),
        ),
        in_specs=[hbm, vmem, vmem, vmem, smem, hbm, hbm, hbm, hbm, hbm],
        out_specs=(vmem, vmem),
        scratch_shapes=[
            pltpu.VMEM((TOK, D), jnp.bfloat16),
            pltpu.VMEM((1, D), jnp.float32),
            pltpu.VMEM((1, D), jnp.float32),
            pltpu.VMEM((D, DD), jnp.bfloat16),
            pltpu.VMEM((8, 256), jnp.int32),
            pltpu.VMEM((NZ, NX, 2 * UNITS, D), jnp.bfloat16),
            pltpu.VMEM((256, D), jnp.bfloat16),
            pltpu.VMEM((EXPERTS, SLOT, WIDE), jnp.bfloat16),
            pltpu.VMEM((EXPERTS, SLOT, WIDE), jnp.bfloat16),
            pltpu.VMEM((EXPERTS, 8, 256), jnp.int32),
            pltpu.VMEM((ROWS, D), jnp.bfloat16),
            pltpu.VMEM((ROWS, D), jnp.float32),
            pltpu.VMEM((EXPERTS, SLOT, DD), jnp.bfloat16),
            pltpu.VMEM((EXPERTS, SLOT, DD), jnp.bfloat16),
            dma((6,)),
            dma((count,)),
            dma((count,)),
            dma((EXPERTS,)),
            dma((EXPERTS,)),
            dma((EXPERTS,)),
            dma((EXPERTS,)),
            dma((EXPERTS,)),
            dma((EXPERTS,)),
        ],
        compiler_params=pltpu.CompilerParams(
            collective_id=0, has_side_effects=True, vmem_limit_bytes=67043328
        ),
    )(*operands)


def decoder_kernel(
    rows_ref, meta_ref, mask_ref, pos_ref, gain_ref, in_ref, out_w_ref, out_ref, start, projected, values_t, mixed
):
    start[:, GRID // 8 * 8 :, :] = jnp.zeros((IMAGES, LANES - GRID // 8 * 8, DD), jnp.float32)
    mask_row = mask_ref[...].astype(jnp.float32).reshape(1, DD)
    position = lax.broadcasted_iota(jnp.int32, (GRID, 256), 0)

    @pl.loop(0, IMAGES)
    def _(i):
        hit = (position == meta_ref[pl.ds(i + 1, 1), :]).astype(jnp.float32)
        covered = jnp.sum(hit, axis=1, keepdims=True)
        placed = jnp.dot(
            hit.astype(jnp.bfloat16), rows_ref[...], preferred_element_type=jnp.float32
        )
        initial = jnp.where(covered > 0.5, placed, mask_row) + pos_ref[...].astype(jnp.float32)
        start[i, 0:GRID, :] = initial
        dec_normed = layer_norm(start[i], gain_ref[...]).astype(jnp.bfloat16)
        product = jnp.dot(dec_normed, in_ref[...], preferred_element_type=jnp.float32)
        projected[i] = product[:, 0 : 2 * DD].astype(jnp.bfloat16)
        values_t[i] = jnp.transpose(product[:, 2 * DD :]).astype(jnp.bfloat16)

    head_lane = lax.div(lax.broadcasted_iota(jnp.int32, (1, 128), 1), HEAD_DIM)
    own_lanes = [(head_lane == h).astype(jnp.float32).astype(jnp.bfloat16) for h in range(4)]
    tail = lax.broadcasted_iota(jnp.int32, (KEYS - FULL, LANES), 0) < GRID - FULL
    exponent = HEAD_DIM ** (-0.5) * 1.4426950408889634

    @pl.loop(0, IMAGES)
    def _(i):
        for g in range(HEADS // 4):
            queries = projected[i, :, g * 128 : (g + 1) * 128]
            keys = projected[i, 0:KEYS, DD + g * 128 : DD + (g + 1) * 128]
            for h in range(4):
                scores = lax.dot_general(
                    keys * own_lanes[h],
                    queries,
                    (((1,), (1,)), ((), ())),
                    preferred_element_type=jnp.float32,
                )
                last = jnp.where(tail, scores[FULL:], -jnp.inf)
                highest = jnp.maximum(
                    jnp.max(scores[:FULL], axis=0, keepdims=True),
                    jnp.max(last, axis=0, keepdims=True),
                )
                raised = jnp.exp2((scores[:FULL] - highest) * exponent)
                raised_last = jnp.exp2((last - highest) * exponent)
                share = 1.0 / (
                    jnp.sum(raised, axis=0, keepdims=True)
                    + jnp.sum(raised_last, axis=0, keepdims=True)
                )
                weights = jnp.concatenate(
                    [(raised * share).astype(jnp.bfloat16), (raised_last * share).astype(jnp.bfloat16)],
                    axis=0,
                )
                first = g * 128 + h * HEAD_DIM
                mixed[first : first + HEAD_DIM, :] = jnp.dot(
                    values_t[i, first : first + HEAD_DIM, 0:KEYS],
                    weights,
                    preferred_element_type=jnp.float32,
                )
        update = jnp.dot(
            jnp.transpose(mixed[...]).astype(jnp.bfloat16),
            out_w_ref[...],
            preferred_element_type=jnp.float32,
        )
        out_ref[i] = (start[i, 0:GRID, :] + update[0:GRID]).astype(jnp.bfloat16)


def decoder_stage(*operands):
    vmem = pl.BlockSpec(memory_space=pltpu.VMEM)
    return pl.pallas_call(
        decoder_kernel,
        out_shape=jax.ShapeDtypeStruct((IMAGES, GRID, DD), jnp.bfloat16),
        in_specs=[vmem] * 7,
        out_specs=vmem,
        scratch_shapes=[
            pltpu.VMEM((IMAGES, LANES, DD), jnp.float32),
            pltpu.VMEM((IMAGES, LANES, 2 * DD), jnp.bfloat16),
            pltpu.VMEM((IMAGES, DD, LANES), jnp.bfloat16),
            pltpu.VMEM((DD, LANES), jnp.float32),
        ],
        compiler_params=pltpu.CompilerParams(vmem_limit_bytes=67043328),
    )(*operands)


def per_device(
    tokens,
    route_weight,
    expert_ids,
    visible,
    owner_map,
    norm_gain,
    expert_in,
    expert_out,
    final_gain,
    embed_weight,
    mask_token,
    decoder_pos,
    decoder_gain,
    attention_in,
    attention_out,
):
    embedded, own_meta = expert_stage(
        tokens,
        route_weight,
        expert_ids.reshape(1, TOK),
        visible,
        owner_map,
        norm_gain.reshape(1, D),
        expert_in,
        expert_out,
        final_gain.reshape(1, D),
        embed_weight,
    )
    return decoder_stage(
        embedded,
        own_meta,
        mask_token,
        decoder_pos,
        decoder_gain.reshape(1, DD),
        attention_in,
        attention_out,
    )


def solution(mesh):
    return jax.shard_map(
        per_device,
        mesh=mesh,
        in_specs=(
            P(("dp", "expert"), None),
            P(("dp", "expert")),
            P(("dp", "expert"), None),
            P(("dp", "expert"), None),
            P(("dp", "expert")),
            P(),
            P("expert", "dp", None),
            P("expert", "dp", None),
            P(),
            P(),
            P(),
            P(),
            P(),
            P(),
            P(),
        ),
        out_specs=P(("dp", "expert"), None, None),
        check_vma=False,
    )
```

```python
import heapq

import jax
import jax.numpy as jnp
from jax import lax
from jax.experimental import pallas as pl
from jax.experimental.pallas import tpu as pltpu
from jax.sharding import PartitionSpec as P

D = 1024
HEADS = 16
HEAD_DIM = 32
DD = 512
GRID = 196
VIS = 49
TOK = 196
EXPERTS = 16
CAP = 24
SLOT = 32
ROWS = EXPERTS * SLOT
WIDE = D + 128
NX = 4
NZ = 8
UNITS = 64
PART = 48
EPSILON = 1e-06
TOKENS_AT = 20.0
IMAGES = 4
LANES = 256
KEYS = 208
FULL = 192


def layer_norm(values, factor):
    values = values.astype(jnp.float32)
    centered = values - jnp.mean(values, axis=-1, keepdims=True)
    variance = jnp.mean(centered * centered, axis=-1, keepdims=True)
    return centered * lax.rsqrt(variance + EPSILON) * factor


def a2_max(j, way):
    return 4 if (way == 1) == (j == 0) else 3


def b1_max(way):
    return 4 if way == 1 else 3


def b2_max(k, way):
    return 2 if (way == 1) == (k % 2 == 0) else 1


def a_from(j):
    return {0: None, 1: ("a1", 0), 2: ("a1", 2), 3: ("a1", 1)}[j]


def z_step(k, longest):
    return (1, k) if k <= longest else (-1, NZ - k)


def build_plan():
    need = {("a1", 0): None, ("a1", 1): None, ("a1", 2): ("a1", 0)}
    for way in (1, -1):
        for t in range(1, b1_max(way) + 1):
            need[("b1", way, t)] = None if t == 1 else ("b1", way, t - 1)
    for k in range(NZ):
        way0, t0 = z_step(k, b1_max(1))
        for way in (1, -1):
            for t in range(1, b2_max(k, way) + 1):
                first = None if k == 0 else ("b1", way0, t0)
                need[("b2", k, way, t)] = first if t == 1 else ("b2", k, way, t - 1)
    for j in range(NX):
        for way in (1, -1):
            for t in range(1, a2_max(j, way) + 1):
                need[("a2", j, way, t)] = a_from(j) if t == 1 else ("a2", j, way, t - 1)

    def link(copy):
        if copy[0] == "a1":
            return ("x", -1 if copy[1] == 1 else 1)
        if copy[0] == "b2":
            return ("x", copy[2])
        return ("z", copy[2] if copy[0] == "a2" else copy[1])

    free = {}
    arrivals = []

    def push(copy, now):
        took = 2.1 if copy[0][0] == "a" else 3.5
        begin = max(now, free.get(link(copy), 0.0))
        free[link(copy)] = begin + took
        heapq.heappush(arrivals, (begin + took + 1.5, len(order) + len(arrivals), copy))

    order = []
    initial = [c for c in need if need[c] is None]
    for copy in initial:
        push(copy, 0.0)
    while arrivals:
        now, _, copy = heapq.heappop(arrivals)
        nexts = [c for c in need if need[c] == copy]
        order.append((now, copy, nexts))
        for c in nexts:
            push(c, now)
    slabs = []
    for k in range(NZ):
        wants = set(("b2", k, way, t) for way in (1, -1) for t in range(1, b2_max(k, way) + 1))
        if k == 0:
            wants |= {("a1", 0), ("a1", 1), ("a1", 2)}
        else:
            wants.add(("b1",) + z_step(k, b1_max(1)))
            for j in range(NX):
                wants.add(("a2", j) + z_step(k, a2_max(j, 1)))
        slabs.append(wants)
    ids = {c: i for i, c in enumerate(need)}
    return initial, order, slabs, ids


def slots_of(ids_row, rows):
    lane = ids_row.shape[1]
    expert = lax.broadcasted_iota(jnp.int32, (EXPERTS, lane), 0)
    onehot = (expert == ids_row).astype(jnp.float32)
    before = (
        lax.broadcasted_iota(jnp.int32, (lane, lane), 0)
        < lax.broadcasted_iota(jnp.int32, (lane, lane), 1)
    ).astype(jnp.bfloat16)
    count = jnp.dot(onehot.astype(jnp.bfloat16), before, preferred_element_type=jnp.float32)
    earlier = jnp.sum(count * onehot, axis=0, keepdims=True).astype(jnp.int32)
    slot = ids_row * SLOT + earlier
    return (lax.broadcasted_iota(jnp.int32, (rows, lane), 0) == slot).astype(jnp.float32)


def gelu(value):
    inner = 0.7978845608028654 * (value + 0.044715 * (value * value * value))
    return 0.5 * value * (1.0 + jnp.tanh(inner))


def expert_kernel(
    tokens_hbm,
    weight_ref,
    ids_ref,
    visible_ref,
    owner_ref,
    gain_hbm,
    in_ref,
    out_ref,
    final_hbm,
    embed_hbm,
    rows_ref,
    own_meta_ref,
    tokens_ref,
    gain_ref,
    final_ref,
    embed_ref,
    meta_ref,
    permute_ref,
    table_ref,
    w,
    tokens_pad,
    send,
    got,
    metas,
    normed,
    total,
    outgoing,
    back,
    local_sems,
    w_send,
    w_recv,
    t_send,
    t_recv,
    m_send,
    m_recv,
    o_send,
    o_recv,
):
    initial, order, slabs, ids = build_plan()
    dp = lax.axis_index("dp")
    me = lax.axis_index("expert")
    z, x = lax.div(dp, NX), lax.rem(dp, NX)

    def at_z(step):
        return lax.rem(z + (step + NZ), NZ)

    def at_x(step):
        return lax.rem(x + (step + NX), NX)

    own_in = pltpu.make_async_copy(in_ref.at[0], w.at[z, x, pl.ds(0, UNITS)], local_sems.at[0])
    own_out = pltpu.make_async_copy(
        out_ref.at[0], w.at[z, x, pl.ds(UNITS, UNITS)], local_sems.at[1]
    )
    own_in.start()
    own_out.start()
    fetches = [
        pltpu.make_async_copy(src, dst, local_sems.at[2 + n])
        for n, (src, dst) in enumerate(
            (
                (tokens_hbm, tokens_ref),
                (gain_hbm, gain_ref),
                (final_hbm, final_ref),
                (embed_hbm, embed_ref),
            )
        )
    ]
    for fetch in fetches:
        fetch.start()
    barrier = pltpu.get_barrier_semaphore()
    for near in (
        at_z(0) * NX + at_x(1),
        at_z(0) * NX + at_x(-1),
        at_z(1) * NX + at_x(0),
        at_z(-1) * NX + at_x(0),
    ):
        pl.semaphore_signal(
            barrier, inc=1, device_id={"dp": near}, device_id_type=pl.DeviceIdType.MESH
        )
    for d in range(1, EXPERTS):
        pl.semaphore_signal(
            barrier,
            inc=1,
            device_id={"expert": lax.rem(me + d, EXPERTS)},
            device_id_type=pl.DeviceIdType.MESH,
        )
    got[:, CAP:SLOT, :] = jnp.zeros((EXPERTS, SLOT - CAP, WIDE), jnp.bfloat16)
    back[:, CAP:SLOT, :] = jnp.zeros((EXPERTS, SLOT - CAP, DD), jnp.bfloat16)
    pad = jnp.full((1, 256 - TOK), -1, jnp.int32)
    meta_ref[0:1, :] = jnp.concatenate([ids_ref[...], pad], axis=1)
    for i in range(IMAGES):
        parts = [visible_ref[i : i + 1, :], jnp.full((1, 256 - VIS * (i + 1)), -1, jnp.int32)]
        if i > 0:
            parts = [jnp.full((1, VIS * i), -1, jnp.int32)] + parts
        meta_ref[i + 1 : i + 2, :] = jnp.concatenate(parts, axis=1)
    meta_ref[5:8, :] = jnp.full((3, 256), owner_ref[0], jnp.int32)
    own_in.wait()
    own_out.wait()
    pl.semaphore_wait(barrier, 4 + EXPERTS - 1)

    def weight_copy(copy, arriving):
        kind = copy[0]
        shift = 1 if arriving else 0
        if kind == "a1":
            step = -1 if copy[1] == 1 else 1
            first = 1 if copy[1] == 2 else 0
            zi, xi = z, at_x(-step * (first + shift))
            target = at_z(0) * NX + at_x(step)
        elif kind == "b2":
            _, k, step, t = copy
            zi, xi = at_z(-k), at_x(-step * (t - 1 + shift))
            target = at_z(0) * NX + at_x(step)
        else:
            step, t = copy[-2:]
            j = copy[1] if kind == "a2" else 0
            zi, xi = at_z(-step * (t - 1 + shift)), at_x(-j)
            target = at_z(step) * NX + at_x(0)
        part = pl.ds(0, PART) if kind[0] == "a" else pl.ds(PART, 2 * UNITS - PART)
        block = w.at[zi, xi, part]
        return pltpu.make_async_remote_copy(
            src_ref=block,
            dst_ref=block,
            send_sem=w_send.at[ids[copy]],
            recv_sem=w_recv.at[ids[copy]],
            device_id={"dp": target},
            device_id_type=pl.DeviceIdType.MESH,
        )

    def exchange(src, dst, send_sem, recv_sem, d, away):
        peer = lax.rem(me + d, EXPERTS)
        from_peer = lax.rem(me + (EXPERTS - d), EXPERTS)
        return pltpu.make_async_remote_copy(
            src_ref=src(peer),
            dst_ref=dst(me if away else from_peer),
            send_sem=send_sem.at[d],
            recv_sem=recv_sem.at[d],
            device_id={"expert": peer},
            device_id_type=pl.DeviceIdType.MESH,
        )

    def meta_copy(d, away):
        return exchange(lambda p: meta_ref, lambda p: metas.at[p], m_send, m_recv, d, away)

    def token_copy(d, away):
        return exchange(
            lambda p: send.at[p, pl.ds(0, CAP)],
            lambda p: got.at[p, pl.ds(0, CAP)],
            t_send,
            t_recv,
            d,
            away,
        )

    def back_copy(d, away):
        return exchange(
            lambda p: outgoing.at[p, pl.ds(0, CAP)],
            lambda p: back.at[p, pl.ds(0, CAP)],
            o_send,
            o_recv,
            d,
            away,
        )

    for copy in initial:
        weight_copy(copy, False).start()
    for d in range(1, EXPERTS):
        meta_copy(d, True).start()
    metas[me] = meta_ref[...]

    for fetch in fetches:
        fetch.wait()
    tokens_pad[TOK // 8 * 8 :, :] = jnp.zeros((256 - TOK // 8 * 8, D), jnp.bfloat16)
    tokens_pad[0:TOK, :] = tokens_ref[...]
    placing = slots_of(meta_ref[0:1, :], ROWS)
    weight_row = jnp.concatenate(
        [weight_ref[...].astype(jnp.float32).reshape(1, TOK), jnp.zeros((1, 256 - TOK), jnp.float32)], axis=1
    )
    scale = jnp.sum(placing * weight_row, axis=1, keepdims=True)
    picked = jnp.dot(
        placing.astype(jnp.bfloat16), tokens_pad[...], preferred_element_type=jnp.float32
    ).astype(jnp.bfloat16)
    send[:, :, 0:D] = picked.reshape(EXPERTS, SLOT, D)
    send[:, :, D:WIDE] = (
        jnp.broadcast_to(scale, (ROWS, 128)).astype(jnp.bfloat16).reshape(EXPERTS, SLOT, 128)
    )
    for d in range(1, EXPERTS):
        token_copy(d, True).start()
    got[me, 0:CAP, :] = send[me, 0:CAP, :]

    def route_back():
        for d in range(1, EXPERTS):
            meta_copy(d, False).wait_recv()
        owners = metas[:, 5, :][:, 0:1]
        lane = lax.broadcasted_iota(jnp.int32, (EXPERTS, ROWS), 1)
        member = lax.broadcasted_iota(jnp.int32, (EXPERTS, ROWS), 0)
        owner_lane = jnp.sum(
            jnp.where(lax.div(lane, SLOT) == member, owners, 0), axis=0, keepdims=True
        )
        row_at = lax.broadcasted_iota(jnp.int32, (ROWS, ROWS), 0)
        lane_at = lax.broadcasted_iota(jnp.int32, (ROWS, ROWS), 1)
        target_row = owner_lane * SLOT + lax.rem(lane_at[0:1, :], SLOT)
        permute_ref[...] = (row_at == target_row).astype(jnp.float32).astype(jnp.bfloat16)
        own_meta = jnp.zeros((8, 256), jnp.int32)
        for s in range(EXPERTS):
            entry = metas[s]
            own_meta = own_meta + jnp.where(entry[5:6, :] == me, entry, 0)
        own_meta_ref[...] = own_meta
        table_ref[...] = jnp.transpose(slots_of(own_meta[0:1, :], ROWS)).astype(jnp.bfloat16)

    def begin_tokens():
        for d in range(1, EXPERTS):
            token_copy(d, False).wait_recv()
        rows = got[:, :, 0:D].reshape(ROWS, D)
        normed[...] = layer_norm(rows, gain_ref[...]).astype(jnp.bfloat16)
        total[...] = jnp.zeros((ROWS, D), jnp.float32)

    def slab(k):
        zi = at_z(-k)

        @pl.loop(0, 2)
        def _(tile):
            part = pl.ds(pl.multiple_of(tile * 256, 256), 256)
            first = w[zi, :, 0:UNITS, :].reshape(NX * UNITS, D)
            second = w[zi, :, UNITS : 2 * UNITS, :].reshape(NX * UNITS, D)
            hidden = gelu(
                lax.dot_general(
                    normed[part, :],
                    first,
                    (((1,), (1,)), ((), ())),
                    preferred_element_type=jnp.float32,
                )
            ).astype(jnp.bfloat16)
            total[part, :] += jnp.dot(hidden, second, preferred_element_type=jnp.float32)

    begun = False
    arrived = set()
    done = set()
    for now, copy, nexts in order:
        weight_copy(copy, True).wait_recv()
        for c in nexts:
            weight_copy(c, False).start()
        arrived.add(copy)
        if not begun and now > TOKENS_AT:
            begin_tokens()
            route_back()
            begun = True
        if begun:
            for k in range(NZ):
                if k not in done and slabs[k] <= arrived:
                    slab(k)
                    done.add(k)

    rows = got[:, :, 0:D].reshape(ROWS, D).astype(jnp.float32)
    scaling = got[:, :, D:WIDE].reshape(ROWS, 128)[:, 0:1].astype(jnp.float32)
    merged = (rows + scaling * total[...]).astype(jnp.bfloat16)
    final_normed = layer_norm(merged, final_ref[...]).astype(jnp.bfloat16)
    embedded = jnp.dot(
        final_normed, embed_ref[...], preferred_element_type=jnp.float32
    ).astype(jnp.bfloat16)
    outgoing[...] = (
        jnp.dot(permute_ref[...], embedded, preferred_element_type=jnp.float32)
        .astype(jnp.bfloat16)
        .reshape(EXPERTS, SLOT, DD)
    )
    for d in range(1, EXPERTS):
        back_copy(d, True).start()
    back[me, 0:CAP, :] = outgoing[me, 0:CAP, :]
    for d in range(1, EXPERTS):
        back_copy(d, False).wait_recv()
    rows_ref[...] = jnp.dot(
        table_ref[...], back[...].reshape(ROWS, DD), preferred_element_type=jnp.float32
    ).astype(jnp.bfloat16)
    for copy in ids:
        weight_copy(copy, False).wait_send()
    for d in range(1, EXPERTS):
        meta_copy(d, True).wait_send()
        token_copy(d, True).wait_send()
        back_copy(d, True).wait_send()


def expert_stage(*operands):
    vmem = pl.BlockSpec(memory_space=pltpu.VMEM)
    hbm = pl.BlockSpec(memory_space=pltpu.HBM)
    smem = pl.BlockSpec(memory_space=pltpu.SMEM)
    count = len(build_plan()[3])
    dma = pltpu.SemaphoreType.DMA
    return pl.pallas_call(
        expert_kernel,
        out_shape=(
            jax.ShapeDtypeStruct((256, DD), jnp.bfloat16),
            jax.ShapeDtypeStruct((8, 256), jnp.int32),
        ),
        in_specs=[hbm, vmem, vmem, vmem, smem, hbm, hbm, hbm, hbm, hbm],
        out_specs=(vmem, vmem),
        scratch_shapes=[
            pltpu.VMEM((TOK, D), jnp.bfloat16),
            pltpu.VMEM((1, D), jnp.float32),
            pltpu.VMEM((1, D), jnp.float32),
            pltpu.VMEM((D, DD), jnp.bfloat16),
            pltpu.VMEM((8, 256), jnp.int32),
            pltpu.VMEM((ROWS, ROWS), jnp.bfloat16),
            pltpu.VMEM((256, ROWS), jnp.bfloat16),
            pltpu.VMEM((NZ, NX, 2 * UNITS, D), jnp.bfloat16),
            pltpu.VMEM((256, D), jnp.bfloat16),
            pltpu.VMEM((EXPERTS, SLOT, WIDE), jnp.bfloat16),
            pltpu.VMEM((EXPERTS, SLOT, WIDE), jnp.bfloat16),
            pltpu.VMEM((EXPERTS, 8, 256), jnp.int32),
            pltpu.VMEM((ROWS, D), jnp.bfloat16),
            pltpu.VMEM((ROWS, D), jnp.float32),
            pltpu.VMEM((EXPERTS, SLOT, DD), jnp.bfloat16),
            pltpu.VMEM((EXPERTS, SLOT, DD), jnp.bfloat16),
            dma((6,)),
            dma((count,)),
            dma((count,)),
            dma((EXPERTS,)),
            dma((EXPERTS,)),
            dma((EXPERTS,)),
            dma((EXPERTS,)),
            dma((EXPERTS,)),
            dma((EXPERTS,)),
        ],
        compiler_params=pltpu.CompilerParams(
            collective_id=0, has_side_effects=True, vmem_limit_bytes=67043328
        ),
    )(*operands)


def decoder_kernel(
    rows_ref, meta_ref, mask_ref, pos_ref, gain_ref, in_ref, out_w_ref, out_ref, start, projected, values_t, mixed
):
    start[:, GRID // 8 * 8 :, :] = jnp.zeros((IMAGES, LANES - GRID // 8 * 8, DD), jnp.float32)
    exponent = HEAD_DIM ** (-0.5) * 1.4426950408889634
    mask_row = mask_ref[...].astype(jnp.float32).reshape(1, DD)
    position = lax.broadcasted_iota(jnp.int32, (GRID, 256), 0)

    @pl.loop(0, IMAGES)
    def _(i):
        hit = (position == meta_ref[pl.ds(i + 1, 1), :]).astype(jnp.float32)
        covered = jnp.sum(hit, axis=1, keepdims=True)
        placed = jnp.dot(
            hit.astype(jnp.bfloat16), rows_ref[...], preferred_element_type=jnp.float32
        )
        initial = jnp.where(covered > 0.5, placed, mask_row) + pos_ref[...].astype(jnp.float32)
        start[i, 0:GRID, :] = initial
        dec_normed = layer_norm(start[i], gain_ref[...]).astype(jnp.bfloat16)
        product = jnp.dot(dec_normed, in_ref[...], preferred_element_type=jnp.float32)
        projected[i, :, 0:DD] = (product[:, 0:DD] * exponent).astype(jnp.bfloat16)
        projected[i, :, DD : 2 * DD] = product[:, DD : 2 * DD].astype(jnp.bfloat16)
        values_t[i] = jnp.transpose(product[:, 2 * DD :]).astype(jnp.bfloat16)

    head_lane = lax.div(lax.broadcasted_iota(jnp.int32, (1, 128), 1), HEAD_DIM)
    own_lanes = [(head_lane == h).astype(jnp.float32).astype(jnp.bfloat16) for h in range(4)]
    tail = lax.broadcasted_iota(jnp.int32, (KEYS - FULL, LANES), 0) < GRID - FULL

    @pl.loop(0, IMAGES)
    def _(i):
        for g in range(HEADS // 4):
            queries = projected[i, :, g * 128 : (g + 1) * 128]
            keys = projected[i, 0:KEYS, DD + g * 128 : DD + (g + 1) * 128]
            for h in range(4):
                scores = lax.dot_general(
                    keys * own_lanes[h],
                    queries,
                    (((1,), (1,)), ((), ())),
                    preferred_element_type=jnp.float32,
                )
                last = jnp.where(tail, scores[FULL:], -jnp.inf)
                highest = jnp.maximum(
                    jnp.max(scores[:FULL], axis=0, keepdims=True),
                    jnp.max(last, axis=0, keepdims=True),
                )
                raised = jnp.exp2(scores[:FULL] - highest)
                raised_last = jnp.exp2(last - highest)
                share = 1.0 / (
                    jnp.sum(raised, axis=0, keepdims=True)
                    + jnp.sum(raised_last, axis=0, keepdims=True)
                )
                weights = jnp.concatenate(
                    [raised.astype(jnp.bfloat16), raised_last.astype(jnp.bfloat16)],
                    axis=0,
                )
                first = g * 128 + h * HEAD_DIM
                summed = jnp.dot(
                    values_t[i, first : first + HEAD_DIM, 0:KEYS],
                    weights,
                    preferred_element_type=jnp.float32,
                )
                mixed[first : first + HEAD_DIM, :] = summed * share
        update = jnp.dot(
            jnp.transpose(mixed[...]).astype(jnp.bfloat16),
            out_w_ref[...],
            preferred_element_type=jnp.float32,
        )
        out_ref[i] = (start[i, 0:GRID, :] + update[0:GRID]).astype(jnp.bfloat16)


def decoder_stage(*operands):
    vmem = pl.BlockSpec(memory_space=pltpu.VMEM)
    return pl.pallas_call(
        decoder_kernel,
        out_shape=jax.ShapeDtypeStruct((IMAGES, GRID, DD), jnp.bfloat16),
        in_specs=[vmem] * 7,
        out_specs=vmem,
        scratch_shapes=[
            pltpu.VMEM((IMAGES, LANES, DD), jnp.float32),
            pltpu.VMEM((IMAGES, LANES, 2 * DD), jnp.bfloat16),
            pltpu.VMEM((IMAGES, DD, LANES), jnp.bfloat16),
            pltpu.VMEM((DD, LANES), jnp.float32),
        ],
        compiler_params=pltpu.CompilerParams(vmem_limit_bytes=67043328),
    )(*operands)


def per_device(
    tokens,
    route_weight,
    expert_ids,
    visible,
    owner_map,
    norm_gain,
    expert_in,
    expert_out,
    final_gain,
    embed_weight,
    mask_token,
    decoder_pos,
    decoder_gain,
    attention_in,
    attention_out,
):
    embedded, own_meta = expert_stage(
        tokens,
        route_weight,
        expert_ids.reshape(1, TOK),
        visible,
        owner_map,
        norm_gain.reshape(1, D),
        expert_in,
        expert_out,
        final_gain.reshape(1, D),
        embed_weight,
    )
    return decoder_stage(
        embedded,
        own_meta,
        mask_token,
        decoder_pos,
        decoder_gain.reshape(1, DD),
        attention_in,
        attention_out,
    )


def solution(mesh):
    return jax.shard_map(
        per_device,
        mesh=mesh,
        in_specs=(
            P(("dp", "expert"), None),
            P(("dp", "expert")),
            P(("dp", "expert"), None),
            P(("dp", "expert"), None),
            P(("dp", "expert")),
            P(),
            P("expert", "dp", None),
            P("expert", "dp", None),
            P(),
            P(),
            P(),
            P(),
            P(),
            P(),
            P(),
        ),
        out_specs=P(("dp", "expert"), None, None),
        check_vma=False,
    )
```

```python
import heapq

import jax
import jax.numpy as jnp
from jax import lax
from jax.experimental import pallas as pl
from jax.experimental.pallas import tpu as pltpu
from jax.sharding import PartitionSpec as P

D = 1024
HEADS = 16
HEAD_DIM = 32
DD = 512
GRID = 196
VIS = 49
TOK = 196
EXPERTS = 16
CAP = 24
SLOT = 32
ROWS = EXPERTS * SLOT
WIDE = D + 128
NX = 4
NZ = 8
UNITS = 64
PART = 48
EPSILON = 1e-06
TOKENS_AT = 26.0
IMAGES = 4
LANES = 256
KEYS = 208
FULL = 192


def layer_norm(values, factor):
    values = values.astype(jnp.float32)
    centered = values - jnp.mean(values, axis=-1, keepdims=True)
    variance = jnp.mean(centered * centered, axis=-1, keepdims=True)
    return centered * lax.rsqrt(variance + EPSILON) * factor


def a2_max(j, way):
    return 4 if (way == 1) == (j == 0) else 3


def b1_max(way):
    return 4 if way == 1 else 3


def b2_max(k, way):
    return 2 if (way == 1) == (k % 2 == 0) else 1


def gate(j):
    return ("b1", 1, {0: 1, 1: 2, 2: 3, 3: 2}[j])


def has_rows(j):
    return {0: None, 1: ("a1", 0), 2: ("a1", 2), 3: ("a1", 1)}[j]


def z_step(k, longest):
    return (1, k) if k <= longest else (-1, NZ - k)


def build_plan():
    need = {("a1", 0): None, ("a1", 1): None, ("a1", 2): ("a1", 0)}
    for way in (1, -1):
        for t in range(1, b1_max(way) + 1):
            need[("b1", way, t)] = None if t == 1 else ("b1", way, t - 1)
    for k in range(NZ):
        way0, t0 = z_step(k, b1_max(1))
        for way in (1, -1):
            for t in range(1, b2_max(k, way) + 1):
                first = None if k == 0 else ("b1", way0, t0)
                need[("b2", k, way, t)] = first if t == 1 else ("b2", k, way, t - 1)
    for j in range(NX):
        for way in (1, -1):
            for t in range(1, a2_max(j, way) + 1):
                need[("a2", j, way, t)] = gate(j) if t == 1 else ("a2", j, way, t - 1)

    def link(copy):
        if copy[0] == "a1":
            return ("x", -1 if copy[1] == 1 else 1)
        if copy[0] == "b2":
            return ("x", copy[2])
        return ("z", copy[2] if copy[0] == "a2" else copy[1])

    free = {}
    arrivals = []

    def push(copy, now):
        took = 2.1 if copy[0][0] == "a" else 3.5
        begin = max(now, free.get(link(copy), 0.0))
        free[link(copy)] = begin + took
        heapq.heappush(arrivals, (begin + took + 1.5, len(order) + len(arrivals), copy))

    order = []
    initial = [c for c in need if need[c] is None]
    for copy in initial:
        push(copy, 0.0)
    while arrivals:
        now, _, copy = heapq.heappop(arrivals)
        nexts = [c for c in need if need[c] == copy]
        order.append((now, copy, nexts))
        seen = [entry[1] for entry in order]
        for c in nexts:
            assert c[0] != "a2" or has_rows(c[1]) is None or has_rows(c[1]) in seen
            push(c, now)
    slabs = []
    for k in range(NZ):
        wants = set(("b2", k, way, t) for way in (1, -1) for t in range(1, b2_max(k, way) + 1))
        if k == 0:
            wants |= {("a1", 0), ("a1", 1), ("a1", 2)}
        else:
            wants.add(("b1",) + z_step(k, b1_max(1)))
            for j in range(NX):
                wants.add(("a2", j) + z_step(k, a2_max(j, 1)))
        slabs.append(wants)
    ids = {c: i for i, c in enumerate(need)}
    return initial, order, slabs, ids


def slots_of(ids_row, rows):
    lane = ids_row.shape[1]
    expert = lax.broadcasted_iota(jnp.int32, (EXPERTS, lane), 0)
    onehot = (expert == ids_row).astype(jnp.float32)
    before = (
        lax.broadcasted_iota(jnp.int32, (lane, lane), 0)
        < lax.broadcasted_iota(jnp.int32, (lane, lane), 1)
    ).astype(jnp.bfloat16)
    count = jnp.dot(onehot.astype(jnp.bfloat16), before, preferred_element_type=jnp.float32)
    earlier = jnp.sum(count * onehot, axis=0, keepdims=True).astype(jnp.int32)
    slot = ids_row * SLOT + earlier
    return (lax.broadcasted_iota(jnp.int32, (rows, lane), 0) == slot).astype(jnp.float32)


def gelu(value):
    inner = 0.7978845608028654 * (value + 0.044715 * (value * value * value))
    return 0.5 * value * (1.0 + jnp.tanh(inner))


def expert_kernel(
    tokens_hbm,
    weight_ref,
    ids_ref,
    visible_ref,
    owner_ref,
    gain_hbm,
    in_ref,
    out_ref,
    final_hbm,
    embed_hbm,
    rows_ref,
    own_meta_ref,
    tokens_ref,
    gain_ref,
    final_ref,
    embed_ref,
    meta_ref,
    permute_ref,
    table_ref,
    w,
    tokens_pad,
    send,
    got,
    metas,
    normed,
    total,
    outgoing,
    back,
    local_sems,
    w_send,
    w_recv,
    t_send,
    t_recv,
    m_send,
    m_recv,
    o_send,
    o_recv,
):
    initial, order, slabs, ids = build_plan()
    dp = lax.axis_index("dp")
    me = lax.axis_index("expert")
    z, x = lax.div(dp, NX), lax.rem(dp, NX)

    def at_z(step):
        return lax.rem(z + (step + NZ), NZ)

    def at_x(step):
        return lax.rem(x + (step + NX), NX)

    own_in = pltpu.make_async_copy(in_ref.at[0], w.at[z, x, pl.ds(0, UNITS)], local_sems.at[0])
    own_out = pltpu.make_async_copy(
        out_ref.at[0], w.at[z, x, pl.ds(UNITS, UNITS)], local_sems.at[1]
    )
    own_in.start()
    own_out.start()
    fetches = [
        pltpu.make_async_copy(src, dst, local_sems.at[2 + n])
        for n, (src, dst) in enumerate(
            (
                (tokens_hbm, tokens_ref),
                (gain_hbm, gain_ref),
                (final_hbm, final_ref),
                (embed_hbm, embed_ref),
            )
        )
    ]
    for fetch in fetches:
        fetch.start()
    barrier = pltpu.get_barrier_semaphore()
    for near in (
        at_z(0) * NX + at_x(1),
        at_z(0) * NX + at_x(-1),
        at_z(1) * NX + at_x(0),
        at_z(-1) * NX + at_x(0),
    ):
        pl.semaphore_signal(
            barrier, inc=1, device_id={"dp": near}, device_id_type=pl.DeviceIdType.MESH
        )
    for d in range(1, EXPERTS):
        pl.semaphore_signal(
            barrier,
            inc=1,
            device_id={"expert": lax.rem(me + d, EXPERTS)},
            device_id_type=pl.DeviceIdType.MESH,
        )
    got[:, CAP:SLOT, :] = jnp.zeros((EXPERTS, SLOT - CAP, WIDE), jnp.bfloat16)
    back[:, CAP:SLOT, :] = jnp.zeros((EXPERTS, SLOT - CAP, DD), jnp.bfloat16)
    pad = jnp.full((1, 256 - TOK), -1, jnp.int32)
    meta_ref[0:1, :] = jnp.concatenate([ids_ref[...], pad], axis=1)
    for i in range(IMAGES):
        parts = [visible_ref[i : i + 1, :], jnp.full((1, 256 - VIS * (i + 1)), -1, jnp.int32)]
        if i > 0:
            parts = [jnp.full((1, VIS * i), -1, jnp.int32)] + parts
        meta_ref[i + 1 : i + 2, :] = jnp.concatenate(parts, axis=1)
    meta_ref[5:8, :] = jnp.full((3, 256), owner_ref[0], jnp.int32)
    own_in.wait()
    own_out.wait()
    pl.semaphore_wait(barrier, 4 + EXPERTS - 1)

    def weight_copy(copy, arriving):
        kind = copy[0]
        shift = 1 if arriving else 0
        if kind == "a1":
            step = -1 if copy[1] == 1 else 1
            first = 1 if copy[1] == 2 else 0
            zi, xi = z, at_x(-step * (first + shift))
            target = at_z(0) * NX + at_x(step)
        elif kind == "b2":
            _, k, step, t = copy
            zi, xi = at_z(-k), at_x(-step * (t - 1 + shift))
            target = at_z(0) * NX + at_x(step)
        else:
            step, t = copy[-2:]
            j = copy[1] if kind == "a2" else 0
            zi, xi = at_z(-step * (t - 1 + shift)), at_x(-j)
            target = at_z(step) * NX + at_x(0)
        part = pl.ds(0, PART) if kind[0] == "a" else pl.ds(PART, 2 * UNITS - PART)
        block = w.at[zi, xi, part]
        return pltpu.make_async_remote_copy(
            src_ref=block,
            dst_ref=block,
            send_sem=w_send.at[ids[copy]],
            recv_sem=w_recv.at[ids[copy]],
            device_id={"dp": target},
            device_id_type=pl.DeviceIdType.MESH,
        )

    def exchange(src, dst, send_sem, recv_sem, d, away):
        peer = lax.rem(me + d, EXPERTS)
        from_peer = lax.rem(me + (EXPERTS - d), EXPERTS)
        return pltpu.make_async_remote_copy(
            src_ref=src(peer),
            dst_ref=dst(me if away else from_peer),
            send_sem=send_sem.at[d],
            recv_sem=recv_sem.at[d],
            device_id={"expert": peer},
            device_id_type=pl.DeviceIdType.MESH,
        )

    def meta_copy(d, away):
        return exchange(lambda p: meta_ref, lambda p: metas.at[p], m_send, m_recv, d, away)

    def token_copy(d, away):
        return exchange(
            lambda p: send.at[p, pl.ds(0, CAP)],
            lambda p: got.at[p, pl.ds(0, CAP)],
            t_send,
            t_recv,
            d,
            away,
        )

    def back_copy(d, away):
        return exchange(
            lambda p: outgoing.at[p, pl.ds(0, CAP)],
            lambda p: back.at[p, pl.ds(0, CAP)],
            o_send,
            o_recv,
            d,
            away,
        )

    for copy in initial:
        weight_copy(copy, False).start()
    for d in range(1, EXPERTS):
        meta_copy(d, True).start()
    metas[me] = meta_ref[...]

    for fetch in fetches:
        fetch.wait()
    tokens_pad[TOK // 8 * 8 :, :] = jnp.zeros((256 - TOK // 8 * 8, D), jnp.bfloat16)
    tokens_pad[0:TOK, :] = tokens_ref[...]
    placing = slots_of(meta_ref[0:1, :], ROWS)
    weight_row = jnp.concatenate(
        [weight_ref[...].astype(jnp.float32).reshape(1, TOK), jnp.zeros((1, 256 - TOK), jnp.float32)], axis=1
    )
    scale = jnp.sum(placing * weight_row, axis=1, keepdims=True)
    picked = jnp.dot(
        placing.astype(jnp.bfloat16), tokens_pad[...], preferred_element_type=jnp.float32
    ).astype(jnp.bfloat16)
    send[:, :, 0:D] = picked.reshape(EXPERTS, SLOT, D)
    send[:, :, D:WIDE] = (
        jnp.broadcast_to(scale, (ROWS, 128)).astype(jnp.bfloat16).reshape(EXPERTS, SLOT, 128)
    )
    for d in range(1, EXPERTS):
        token_copy(d, True).start()
    got[me, 0:CAP, :] = send[me, 0:CAP, :]

    def route_back():
        for d in range(1, EXPERTS):
            meta_copy(d, False).wait_recv()
        owners = metas[:, 5, :][:, 0:1]
        lane = lax.broadcasted_iota(jnp.int32, (EXPERTS, ROWS), 1)
        member = lax.broadcasted_iota(jnp.int32, (EXPERTS, ROWS), 0)
        owner_lane = jnp.sum(
            jnp.where(lax.div(lane, SLOT) == member, owners, 0), axis=0, keepdims=True
        )
        row_at = lax.broadcasted_iota(jnp.int32, (ROWS, ROWS), 0)
        lane_at = lax.broadcasted_iota(jnp.int32, (ROWS, ROWS), 1)
        target_row = owner_lane * SLOT + lax.rem(lane_at[0:1, :], SLOT)
        permute_ref[...] = (row_at == target_row).astype(jnp.float32).astype(jnp.bfloat16)
        own_meta = jnp.zeros((8, 256), jnp.int32)
        for s in range(EXPERTS):
            entry = metas[s]
            own_meta = own_meta + jnp.where(entry[5:6, :] == me, entry, 0)
        own_meta_ref[...] = own_meta
        table_ref[...] = jnp.transpose(slots_of(own_meta[0:1, :], ROWS)).astype(jnp.bfloat16)

    def begin_tokens():
        for d in range(1, EXPERTS):
            token_copy(d, False).wait_recv()
        rows = got[:, :, 0:D].reshape(ROWS, D)
        normed[...] = layer_norm(rows, gain_ref[...]).astype(jnp.bfloat16)
        total[...] = jnp.zeros((ROWS, D), jnp.float32)

    def slab(k):
        zi = at_z(-k)

        @pl.loop(0, 2)
        def _(tile):
            part = pl.ds(pl.multiple_of(tile * 256, 256), 256)
            first = w[zi, :, 0:UNITS, :].reshape(NX * UNITS, D)
            second = w[zi, :, UNITS : 2 * UNITS, :].reshape(NX * UNITS, D)
            hidden = gelu(
                lax.dot_general(
                    normed[part, :],
                    first,
                    (((1,), (1,)), ((), ())),
                    preferred_element_type=jnp.float32,
                )
            ).astype(jnp.bfloat16)
            total[part, :] += jnp.dot(hidden, second, preferred_element_type=jnp.float32)

    begun = False
    arrived = set()
    done = set()
    for now, copy, nexts in order:
        weight_copy(copy, True).wait_recv()
        for c in nexts:
            weight_copy(c, False).start()
        arrived.add(copy)
        if not begun and now > TOKENS_AT:
            begin_tokens()
            route_back()
            begun = True
        if begun:
            for k in range(NZ):
                if k not in done and slabs[k] <= arrived:
                    slab(k)
                    done.add(k)

    rows = got[:, :, 0:D].reshape(ROWS, D).astype(jnp.float32)
    scaling = got[:, :, D:WIDE].reshape(ROWS, 128)[:, 0:1].astype(jnp.float32)
    merged = (rows + scaling * total[...]).astype(jnp.bfloat16)
    final_normed = layer_norm(merged, final_ref[...]).astype(jnp.bfloat16)
    embedded = jnp.dot(
        final_normed, embed_ref[...], preferred_element_type=jnp.float32
    ).astype(jnp.bfloat16)
    outgoing[...] = (
        jnp.dot(permute_ref[...], embedded, preferred_element_type=jnp.float32)
        .astype(jnp.bfloat16)
        .reshape(EXPERTS, SLOT, DD)
    )
    for d in range(1, EXPERTS):
        back_copy(d, True).start()
    back[me, 0:CAP, :] = outgoing[me, 0:CAP, :]
    for d in range(1, EXPERTS):
        back_copy(d, False).wait_recv()
    rows_ref[...] = jnp.dot(
        table_ref[...], back[...].reshape(ROWS, DD), preferred_element_type=jnp.float32
    ).astype(jnp.bfloat16)
    for copy in ids:
        weight_copy(copy, False).wait_send()
    for d in range(1, EXPERTS):
        meta_copy(d, True).wait_send()
        token_copy(d, True).wait_send()
        back_copy(d, True).wait_send()


def expert_stage(*operands):
    vmem = pl.BlockSpec(memory_space=pltpu.VMEM)
    hbm = pl.BlockSpec(memory_space=pltpu.HBM)
    smem = pl.BlockSpec(memory_space=pltpu.SMEM)
    count = len(build_plan()[3])
    dma = pltpu.SemaphoreType.DMA
    return pl.pallas_call(
        expert_kernel,
        out_shape=(
            jax.ShapeDtypeStruct((256, DD), jnp.bfloat16),
            jax.ShapeDtypeStruct((8, 256), jnp.int32),
        ),
        in_specs=[hbm, vmem, vmem, vmem, smem, hbm, hbm, hbm, hbm, hbm],
        out_specs=(vmem, vmem),
        scratch_shapes=[
            pltpu.VMEM((TOK, D), jnp.bfloat16),
            pltpu.VMEM((1, D), jnp.float32),
            pltpu.VMEM((1, D), jnp.float32),
            pltpu.VMEM((D, DD), jnp.bfloat16),
            pltpu.VMEM((8, 256), jnp.int32),
            pltpu.VMEM((ROWS, ROWS), jnp.bfloat16),
            pltpu.VMEM((256, ROWS), jnp.bfloat16),
            pltpu.VMEM((NZ, NX, 2 * UNITS, D), jnp.bfloat16),
            pltpu.VMEM((256, D), jnp.bfloat16),
            pltpu.VMEM((EXPERTS, SLOT, WIDE), jnp.bfloat16),
            pltpu.VMEM((EXPERTS, SLOT, WIDE), jnp.bfloat16),
            pltpu.VMEM((EXPERTS, 8, 256), jnp.int32),
            pltpu.VMEM((ROWS, D), jnp.bfloat16),
            pltpu.VMEM((ROWS, D), jnp.float32),
            pltpu.VMEM((EXPERTS, SLOT, DD), jnp.bfloat16),
            pltpu.VMEM((EXPERTS, SLOT, DD), jnp.bfloat16),
            dma((6,)),
            dma((count,)),
            dma((count,)),
            dma((EXPERTS,)),
            dma((EXPERTS,)),
            dma((EXPERTS,)),
            dma((EXPERTS,)),
            dma((EXPERTS,)),
            dma((EXPERTS,)),
        ],
        compiler_params=pltpu.CompilerParams(
            collective_id=0, has_side_effects=True, vmem_limit_bytes=67043328
        ),
    )(*operands)


def decoder_kernel(
    rows_ref, meta_ref, mask_ref, pos_ref, gain_ref, in_ref, out_w_ref, out_ref, start, projected, values_t, mixed
):
    start[:, GRID // 8 * 8 :, :] = jnp.zeros((IMAGES, LANES - GRID // 8 * 8, DD), jnp.float32)
    exponent = HEAD_DIM ** (-0.5) * 1.4426950408889634
    mask_row = mask_ref[...].astype(jnp.float32).reshape(1, DD)
    position = lax.broadcasted_iota(jnp.int32, (GRID, 256), 0)

    @pl.loop(0, IMAGES)
    def _(i):
        hit = (position == meta_ref[pl.ds(i + 1, 1), :]).astype(jnp.float32)
        covered = jnp.sum(hit, axis=1, keepdims=True)
        placed = jnp.dot(
            hit.astype(jnp.bfloat16), rows_ref[...], preferred_element_type=jnp.float32
        )
        initial = jnp.where(covered > 0.5, placed, mask_row) + pos_ref[...].astype(jnp.float32)
        start[i, 0:GRID, :] = initial
        dec_normed = layer_norm(start[i], gain_ref[...]).astype(jnp.bfloat16)
        product = jnp.dot(dec_normed, in_ref[...], preferred_element_type=jnp.float32)
        projected[i, :, 0:DD] = (product[:, 0:DD] * exponent).astype(jnp.bfloat16)
        projected[i, :, DD : 2 * DD] = product[:, DD : 2 * DD].astype(jnp.bfloat16)
        values_t[i] = jnp.transpose(product[:, 2 * DD :]).astype(jnp.bfloat16)

    head_lane = lax.div(lax.broadcasted_iota(jnp.int32, (1, 128), 1), HEAD_DIM)
    own_lanes = [(head_lane == h).astype(jnp.float32).astype(jnp.bfloat16) for h in range(4)]
    tail = lax.broadcasted_iota(jnp.int32, (KEYS - FULL, LANES), 0) < GRID - FULL

    @pl.loop(0, IMAGES)
    def _(i):
        for g in range(HEADS // 4):
            queries = projected[i, :, g * 128 : (g + 1) * 128]
            keys = projected[i, 0:KEYS, DD + g * 128 : DD + (g + 1) * 128]
            for h in range(4):
                scores = lax.dot_general(
                    keys * own_lanes[h],
                    queries,
                    (((1,), (1,)), ((), ())),
                    preferred_element_type=jnp.float32,
                )
                last = jnp.where(tail, scores[FULL:], -jnp.inf)
                highest = jnp.maximum(
                    jnp.max(scores[:FULL], axis=0, keepdims=True),
                    jnp.max(last, axis=0, keepdims=True),
                )
                raised = jnp.exp2(scores[:FULL] - highest)
                raised_last = jnp.exp2(last - highest)
                share = 1.0 / (
                    jnp.sum(raised, axis=0, keepdims=True)
                    + jnp.sum(raised_last, axis=0, keepdims=True)
                )
                weights = jnp.concatenate(
                    [raised.astype(jnp.bfloat16), raised_last.astype(jnp.bfloat16)],
                    axis=0,
                )
                first = g * 128 + h * HEAD_DIM
                summed = jnp.dot(
                    values_t[i, first : first + HEAD_DIM, 0:KEYS],
                    weights,
                    preferred_element_type=jnp.float32,
                )
                mixed[first : first + HEAD_DIM, :] = summed * share
        update = jnp.dot(
            jnp.transpose(mixed[...]).astype(jnp.bfloat16),
            out_w_ref[...],
            preferred_element_type=jnp.float32,
        )
        out_ref[i] = (start[i, 0:GRID, :] + update[0:GRID]).astype(jnp.bfloat16)


def decoder_stage(*operands):
    vmem = pl.BlockSpec(memory_space=pltpu.VMEM)
    return pl.pallas_call(
        decoder_kernel,
        out_shape=jax.ShapeDtypeStruct((IMAGES, GRID, DD), jnp.bfloat16),
        in_specs=[vmem] * 7,
        out_specs=vmem,
        scratch_shapes=[
            pltpu.VMEM((IMAGES, LANES, DD), jnp.float32),
            pltpu.VMEM((IMAGES, LANES, 2 * DD), jnp.bfloat16),
            pltpu.VMEM((IMAGES, DD, LANES), jnp.bfloat16),
            pltpu.VMEM((DD, LANES), jnp.float32),
        ],
        compiler_params=pltpu.CompilerParams(vmem_limit_bytes=67043328),
    )(*operands)


def per_device(
    tokens,
    route_weight,
    expert_ids,
    visible,
    owner_map,
    norm_gain,
    expert_in,
    expert_out,
    final_gain,
    embed_weight,
    mask_token,
    decoder_pos,
    decoder_gain,
    attention_in,
    attention_out,
):
    embedded, own_meta = expert_stage(
        tokens,
        route_weight,
        expert_ids.reshape(1, TOK),
        visible,
        owner_map,
        norm_gain.reshape(1, D),
        expert_in,
        expert_out,
        final_gain.reshape(1, D),
        embed_weight,
    )
    return decoder_stage(
        embedded,
        own_meta,
        mask_token,
        decoder_pos,
        decoder_gain.reshape(1, DD),
        attention_in,
        attention_out,
    )


def solution(mesh):
    return jax.shard_map(
        per_device,
        mesh=mesh,
        in_specs=(
            P(("dp", "expert"), None),
            P(("dp", "expert")),
            P(("dp", "expert"), None),
            P(("dp", "expert"), None),
            P(("dp", "expert")),
            P(),
            P("expert", "dp", None),
            P("expert", "dp", None),
            P(),
            P(),
            P(),
            P(),
            P(),
            P(),
            P(),
        ),
        out_specs=P(("dp", "expert"), None, None),
        check_vma=False,
    )
```
